32 devices in a mesh: shard: 2 (over x), ctx: 2 (over core), tensor: 8 (over z, y).
Axes of the slice: x: 2, y: 2, z: 4, core: 2. Of those that a mesh axis runs over, the one named last changes fastest.
Arguments:
- inputs: bfloat16 [2, 1024, 1152], P('shard', 'ctx'), may hold values from -6 to 6
- cotangent: bfloat16 [2, 1024, 1152], P('shard', 'ctx'), may hold values from -6 to 6
- attn_norm_gain: float32 [1152], replicated, may hold values from 0.1 to 1.9
- attn_norm_bias: float32 [1152], replicated, may hold values from -0.1875 to 0.1875
- qkv_weight: bfloat16 [3, 1152, 1152], P(None, 'shard', 'tensor'), may hold values from -0.8249579 to 0.8249579
- query_value_bias: float32 [2, 1152], P(None, 'tensor'), may hold values from -1.8 to 1.8
- out_weight: bfloat16 [1152, 1152], P('tensor', 'shard'), may hold values from -4 to 4
- out_bias: float32 [1152], replicated, may hold values from -1.75 to 1.75
- mlp_norm_gain: float32 [1152], replicated, may hold values from 0.1 to 1.9
- mlp_norm_bias: float32 [1152], replicated, may hold values from -1.75 to 1.75
- up_weight: bfloat16 [1152, 4304], P('shard', 'tensor'), may hold values from -0.1875 to 0.1875
- up_bias: float32 [4304], P('tensor'), may hold values from -1.75 to 1.75
- down_weight: bfloat16 [4304, 1152], P('tensor', 'shard'), may hold values from -0.1875 to 0.1875
- down_bias: float32 [1152], replicated, may hold values from -1.75 to 1.75
Outputs:
- output: bfloat16 [2, 1024, 1152], P('shard', 'ctx')
- inputs_grad: float32 [2, 1024, 1152], P('shard', 'ctx')
- attn_norm_gain_grad: float32 [1152], replicated
- attn_norm_bias_grad: float32 [1152], replicated
- qkv_weight_grad: float32 [3, 1152, 1152], P(None, 'shard', 'tensor')
- query_value_bias_grad: float32 [2, 1152], P(None, 'tensor')
- out_weight_grad: float32 [1152, 1152], P('tensor', 'shard')
- out_bias_grad: float32 [1152], replicated
- mlp_norm_gain_grad: float32 [1152], replicated
- mlp_norm_bias_grad: float32 [1152], replicated
- up_weight_grad: float32 [1152, 4304], P('shard', 'tensor')
- up_bias_grad: float32 [4304], P('tensor')
- down_weight_grad: float32 [4304, 1152], P('tensor', 'shard')
- down_bias_grad: float32 [1152], replicated
The draws below stay inside these ranges and needn't reach their ends.
All inputs are finite; a program needn't handle non-finite values.
Results may differ from the reference program's by a relative error of at most 0.023.
Values may be sent and summed in bfloat16 or wider, within the bound.
No kernel may reach another device: no remote copies, remote signals or barrier semaphores. Data moves between devices by JAX's collectives and lax.ppermute only.
A program may use at most 128 MiB of HBM per device.

```python
import jax
import jax.numpy as jnp
from jax import lax

D = 1152
H = 16
HD = 72
FF = 4304
SEQ = 1024
IMAGES = 2
N_TENSOR = 8


def draw_qkv_weight(key, part):
    key_base = jax.random.fold_in(key, 11)
    scaling = D ** (-0.5)
    base = jnp.clip(jax.random.normal(key_base, (3, D, H * HD), jnp.float32), -6.0, 6.0) * scaling
    return base.astype(jnp.bfloat16)


def draw_query_value_bias(key, part):
    key_bias = jax.random.fold_in(key, 37)
    row_scales = jnp.array([0.3, 0.03], jnp.float32)[:, None]
    base = jnp.clip(jax.random.normal(key_bias, (2, H * HD), jnp.float32), -6.0, 6.0)
    return (base * row_scales).astype(jnp.float32)


def shard_levels(rng, shape, cuts, low, largest):
    factor_of, own = 1.0, jax.random.fold_in(rng, 6)
    for dim, parts in cuts:
        draws = jnp.exp(jax.random.uniform(jax.random.fold_in(own, dim), (parts,), jnp.float32, low / len(cuts), largest / len(cuts)))
        factor_of = factor_of * jnp.repeat(draws, shape[dim] // parts).reshape([-1 if axis == dim else 1 for axis in range(len(shape))])
    return factor_of


def gaussian(key, dims, scale, limit, shards=(), kind=jnp.bfloat16):
    level = shard_levels(key, dims, shards, -0.22, 0.18) if shards else 1.0
    drawn = jax.random.normal(key, dims, jnp.float32) * scale * level
    return jnp.minimum(jnp.maximum(drawn, -limit), limit).astype(kind)


def setup_inputs(seed: int = 0) -> dict:
    streams_of = jax.random.split(jax.random.key(seed), 15)
    inputs = gaussian(streams_of[0], (IMAGES, SEQ, D), 1.0, 6.0, ((0, 2), (1, 2)))
    cotangent = gaussian(streams_of[1], (IMAGES, SEQ, D), 1.0, 6.0, ((0, 2), (1, 2)))
    attn_norm_gain = jnp.clip(1.0 + 0.18 * jax.random.normal(streams_of[2], (D,), jnp.float32), 0.1, 1.9)
    attn_norm_bias = gaussian(streams_of[3], (D,), 0.03, 0.1875, (), jnp.float32)
    qkv_weight = draw_qkv_weight(jax.random.fold_in(streams_of[14], 71), 0)
    query_value_bias = draw_query_value_bias(jax.random.fold_in(streams_of[14], 71), 0)
    out_weight = gaussian(streams_of[6], (H * HD, D), ((SEQ * 0.5) ** 0.5 * (H * HD) ** -0.5), 4.0, ((0, 8), (1, 2)))
    out_bias = gaussian(streams_of[7], (D,), 0.3, 1.75, (), jnp.float32)
    mlp_norm_gain = jnp.clip(1.0 + 0.18 * jax.random.normal(streams_of[8], (D,), jnp.float32), 0.1, 1.9)
    mlp_norm_bias = gaussian(streams_of[9], (D,), 0.3, 1.75, (), jnp.float32)
    up_weight = gaussian(streams_of[10], (D, FF), D ** -0.5, 0.1875, ((0, 2), (1, 8)))
    up_bias = gaussian(streams_of[11], (FF,), 0.3, 1.75, ((0, 8),), jnp.float32)
    down_weight = gaussian(streams_of[12], (FF, D), (2.0 * FF ** -0.5), 0.1875, ((0, 8), (1, 2)))
    down_bias = gaussian(streams_of[13], (D,), 0.3, 1.75, (), jnp.float32)
    return dict(inputs=inputs, cotangent=cotangent, attn_norm_gain=attn_norm_gain, attn_norm_bias=attn_norm_bias, qkv_weight=qkv_weight, query_value_bias=query_value_bias, out_weight=out_weight, out_bias=out_bias, mlp_norm_gain=mlp_norm_gain, mlp_norm_bias=mlp_norm_bias, up_weight=up_weight, up_bias=up_bias, down_weight=down_weight, down_bias=down_bias)


EPSILON = 1e-06

def layer_norm(rows, gain, shift):
    center = lax.optimization_barrier(jnp.mean(rows, axis=-1, keepdims=True))
    offset = rows - center
    spread = lax.optimization_barrier(jnp.mean(offset * offset, axis=-1, keepdims=True))
    return offset * lax.rsqrt(spread + EPSILON) * gain + shift

def gelu_tanh(values):
    return jax.nn.gelu(values, approximate=True)

def product(left, right):
    return jnp.dot(left, right, preferred_element_type=jnp.float32)

def rounded_sum(partials):
    total = jnp.zeros(partials[0].shape, jnp.float32)
    for partial_term in partials:
        total = total + lax.optimization_barrier(partial_term.astype(jnp.bfloat16)).astype(jnp.float32)
    return total

def head_forward(operands):
    queries, keys, values = operands
    scores = product(queries, keys.T) * HD ** (-0.5)
    row_max = lax.optimization_barrier(jnp.max(scores, axis=1, keepdims=True))
    unscaled = jnp.exp(scores - row_max)
    totals = lax.optimization_barrier(jnp.sum(unscaled, axis=1, keepdims=True))
    attended = product(unscaled.astype(jnp.bfloat16), values) / totals
    return (attended, row_max + jnp.log(totals))

def head_backward(operands):
    queries, keys, values, d_attended, attended_b, log_total = operands
    scaling = HD ** (-0.5)
    scores = product(queries, keys.T) * scaling
    probs = jnp.exp(scores - log_total)
    delta = lax.optimization_barrier(jnp.sum(d_attended.astype(jnp.float32) * attended_b.astype(jnp.float32), axis=1, keepdims=True))
    d_scores = probs * (product(d_attended, values.T) - delta)
    scores_b = d_scores.astype(jnp.bfloat16)
    d_queries = product(scores_b, keys) * scaling
    d_keys = product(scores_b.T, queries) * scaling
    d_values = product(probs.astype(jnp.bfloat16).T, d_attended)
    return (d_queries, d_keys, d_values)

def image_pass(rows_bf, upstream, params):
    attn_norm_gain, attn_norm_bias, qkv_weight, query_value_bias, out_weight, out_bias, mlp_norm_gain, mlp_norm_bias, up_weight, up_bias, down_weight, down_bias = params
    seq_rows = rows_bf.shape[0]
    head_group = H * HD // N_TENSOR
    unit_group = FF // N_TENSOR

    def to_heads(matrix):
        return matrix.reshape(seq_rows, H, HD).transpose(1, 0, 2)

    def from_heads(tensor):
        return tensor.transpose(1, 0, 2).reshape(seq_rows, H * HD)
    rows_in = rows_bf.astype(jnp.float32)
    upstream_f = upstream.astype(jnp.float32)
    normed_one, norm_one_back = jax.vjp(layer_norm, rows_in, attn_norm_gain, attn_norm_bias)
    attn_in = normed_one.astype(jnp.bfloat16)
    queries = (product(attn_in, qkv_weight[0]) + query_value_bias[0]).astype(jnp.bfloat16)
    keys = product(attn_in, qkv_weight[1]).astype(jnp.bfloat16)
    values = (product(attn_in, qkv_weight[2]) + query_value_bias[1]).astype(jnp.bfloat16)
    attended, log_total = lax.map(head_forward, (to_heads(queries), to_heads(keys), to_heads(values)))
    attended_b = from_heads(attended).astype(jnp.bfloat16)
    attn_sum = rounded_sum([product(attended_b[:, group * head_group:(group + 1) * head_group], out_weight[group * head_group:(group + 1) * head_group]) for group in range(N_TENSOR)])
    residual = rows_in + attn_sum + out_bias
    normed_two, norm_two_back = jax.vjp(layer_norm, residual, mlp_norm_gain, mlp_norm_bias)
    mlp_in = normed_two.astype(jnp.bfloat16)
    hidden = product(mlp_in, up_weight) + up_bias
    activ_f, gelu_back = jax.vjp(gelu_tanh, hidden)
    activated = activ_f.astype(jnp.bfloat16)
    mlp_sum = rounded_sum([product(activated[:, group * unit_group:(group + 1) * unit_group], down_weight[group * unit_group:(group + 1) * unit_group]) for group in range(N_TENSOR)])
    output = (residual + mlp_sum + down_bias).astype(jnp.bfloat16)
    down_bias_grad = lax.optimization_barrier(jnp.sum(upstream_f, axis=0))
    down_weight_grad = product(activated.T, upstream)
    d_hidden, = gelu_back(product(upstream, down_weight.T))
    up_bias_grad = lax.optimization_barrier(jnp.sum(d_hidden, axis=0))
    d_hidden_b = d_hidden.astype(jnp.bfloat16)
    up_weight_grad = product(mlp_in.T, d_hidden_b)
    d_mlp_in = rounded_sum([product(d_hidden_b[:, group * unit_group:(group + 1) * unit_group], up_weight[:, group * unit_group:(group + 1) * unit_group].T) for group in range(N_TENSOR)])
    d_norm_two, mlp_norm_gain_grad, mlp_norm_bias_grad = norm_two_back(d_mlp_in)
    d_residual = upstream_f + d_norm_two
    out_bias_grad = lax.optimization_barrier(jnp.sum(d_residual, axis=0))
    d_residual_b = d_residual.astype(jnp.bfloat16)
    out_weight_grad = product(attended_b.T, d_residual_b)
    d_attended = product(d_residual_b, out_weight.T).astype(jnp.bfloat16)
    d_queries, d_keys, d_values = lax.map(head_backward, (to_heads(queries), to_heads(keys), to_heads(values), to_heads(d_attended), to_heads(attended_b), log_total))
    d_queries = from_heads(d_queries)
    d_keys = from_heads(d_keys)
    d_values = from_heads(d_values)
    query_value_bias_grad = jnp.stack([lax.optimization_barrier(jnp.sum(d_queries, axis=0)), lax.optimization_barrier(jnp.sum(d_values, axis=0))])
    d_proj = [d_queries.astype(jnp.bfloat16), d_keys.astype(jnp.bfloat16), d_values.astype(jnp.bfloat16)]
    qkv_weight_grad = jnp.stack([product(attn_in.T, d_proj[index]) for index in range(3)])
    partials = []
    for group in range(N_TENSOR):
        window = slice(group * head_group, (group + 1) * head_group)
        partial_term = product(d_proj[0][:, window], qkv_weight[0][:, window].T)
        partial_term = partial_term + product(d_proj[1][:, window], qkv_weight[1][:, window].T)
        partial_term = partial_term + product(d_proj[2][:, window], qkv_weight[2][:, window].T)
        partials.append(partial_term)
    d_attn_in = rounded_sum(partials)
    d_norm_one, attn_norm_gain_grad, attn_norm_bias_grad = norm_one_back(d_attn_in)
    inputs_grad = d_residual + d_norm_one
    grads = (attn_norm_gain_grad, attn_norm_bias_grad, qkv_weight_grad, query_value_bias_grad, out_weight_grad, out_bias_grad, mlp_norm_gain_grad, mlp_norm_bias_grad, up_weight_grad, up_bias_grad, down_weight_grad, down_bias_grad)
    return (output, inputs_grad, grads)

def reference(inputs, cotangent, attn_norm_gain, attn_norm_bias, qkv_weight, query_value_bias, out_weight, out_bias, mlp_norm_gain, mlp_norm_bias, up_weight, up_bias, down_weight, down_bias):
    params = (attn_norm_gain, attn_norm_bias, qkv_weight, query_value_bias, out_weight, out_bias, mlp_norm_gain, mlp_norm_bias, up_weight, up_bias, down_weight, down_bias)
    outputs = []
    input_grads = []
    summed = None
    for image in range(IMAGES):
        output, inputs_grad, grads = image_pass(inputs[image], cotangent[image], params)
        outputs.append(output)
        input_grads.append(inputs_grad)
        summed = grads if summed is None else jax.tree.map(lambda first, second: first + second, summed, grads)
    return (jnp.stack(outputs), jnp.stack(input_grads), summed[0], summed[1], summed[2], summed[3], summed[4], summed[5], summed[6], summed[7], summed[8], summed[9], summed[10], summed[11])
```

```python
import jax
import jax.numpy as jnp
from jax import lax
from jax.sharding import PartitionSpec as P

HD = 72


EPSILON = 1e-06


def layer_norm(rows, gain, shift):
    center = jnp.mean(rows, axis=-1, keepdims=True)
    offset = rows - center
    spread = jnp.mean(offset * offset, axis=-1, keepdims=True)
    return offset * lax.rsqrt(spread + EPSILON) * gain + shift


def gelu_tanh(values):
    return jax.nn.gelu(values, approximate=True)


def product(left, right):
    return jnp.dot(left, right, preferred_element_type=jnp.float32)


def split_heads(matrix):
    return matrix.reshape(matrix.shape[0], -1, HD)

BF16 = jnp.bfloat16
F32 = jnp.float32


def swap(array, axis, mask):
    count = lax.axis_size(axis)
    return lax.ppermute(array, axis, [(i, i ^ mask) for i in range(count)])


def bits_of(axis):
    count = lax.axis_size(axis)
    return [1 << b for b in range(count.bit_length() - 1)]


def take_bit(blocks, bits, mask):
    place = bits.index(mask)
    tail_shape = blocks.shape[1:]
    grid = blocks.reshape((2,) * len(bits) + tail_shape)
    low = lax.index_in_dim(grid, 0, place, False).reshape((-1,) + tail_shape)
    high = lax.index_in_dim(grid, 1, place, False).reshape((-1,) + tail_shape)
    return low, high, [b for b in bits if b != mask]


def orders_of(bits):
    first = list(bits)
    second = list(bits)
    if len(bits) > 2:
        second[0], second[1] = second[1], second[0]
    return first, second


def scatter_part(blocks, bits, order):
    for mask in order:
        low, high, bits = take_bit(blocks, bits, mask)
        arrived = swap(high, "tensor", mask)
        blocks = (low.astype(F32) + arrived.astype(F32)).astype(BF16)
    return blocks[0]


def reduce_scatter(partial, parts=2):
    bits = bits_of("tensor")
    count = 1 << len(bits)
    rows = partial.shape[0] // count
    blocks = partial.reshape(count, rows, -1)
    high_first = bits[::-1]
    orders = orders_of(bits)
    step = rows // parts
    done = [
        scatter_part(blocks[:, p * step : (p + 1) * step], high_first, orders[p % 2])
        for p in range(parts)
    ]
    return jnp.concatenate(done, axis=0)


def gather_part(block, order):
    bits = []
    blocks = block[None]
    for mask in order:
        arrived = swap(blocks, "tensor", mask)
        blocks = jnp.concatenate([blocks, arrived], axis=0)
        bits = [mask] + bits
    tail_shape = blocks.shape[1:]
    want = sorted(bits, reverse=True)
    grid = blocks.reshape((2,) * len(bits) + tail_shape)
    axes = [bits.index(b) for b in want] + [len(bits) + d for d in range(len(tail_shape))]
    return grid.transpose(axes).reshape((-1,) + tail_shape)


def gather(block, parts=2):
    orders = [order[::-1] for order in orders_of(bits_of("tensor"))]
    step = block.shape[0] // parts
    done = [gather_part(block[p * step : (p + 1) * step], orders[p % 2]) for p in range(parts)]
    full = jnp.concatenate(done, axis=1)
    return full.reshape(-1, full.shape[-1])


def relative(rows):
    index = lax.axis_index("tensor")
    bits = bits_of("tensor")[::-1]
    tail_shape = (rows.shape[0] >> len(bits),) + rows.shape[1:]
    grid = rows.reshape((2,) * len(bits) + tail_shape)
    for place, mask in enumerate(bits):
        grid = jnp.where((index & mask) != 0, jnp.flip(grid, place), grid)
    return grid.reshape(rows.shape)


def pick(flag, first, second):
    return jnp.where(flag, first, second)


def ctx_rest(array):
    for mask in bits_of("ctx")[1:]:
        array = array + swap(array, "ctx", mask)
    return array


def on_device(
    inputs,
    cotangent,
    attn_norm_gain,
    attn_norm_bias,
    qkv_weight,
    query_value_bias,
    out_weight,
    out_bias,
    mlp_norm_gain,
    mlp_norm_bias,
    up_weight,
    up_bias,
    down_weight,
    down_bias,
):
    width = inputs.shape[-1]
    half = width // 2
    heads_width = qkv_weight.shape[-1]
    units = up_weight.shape[-1]
    shard = lax.axis_index("shard")
    core = lax.axis_index("ctx") & 1
    first_shard = shard == 0
    first_core = core == 0
    scaling = HD ** (-0.5)

    quarter = half // 2
    qkv_sent = lax.dynamic_slice_in_dim(qkv_weight, core * quarter, quarter, 1)
    qkv_here = swap(qkv_sent, "shard", 1)
    qkv_there = swap(qkv_here, "ctx", 1)
    qkv_other = jnp.concatenate(
        [pick(first_core, qkv_here, qkv_there), pick(first_core, qkv_there, qkv_here)], axis=1
    )
    qkv_full = jnp.concatenate(
        [pick(first_shard, qkv_weight, qkv_other), pick(first_shard, qkv_other, qkv_weight)],
        axis=1,
    )
    out_other = swap(out_weight, "shard", 1)
    out_full = jnp.concatenate(
        [pick(first_shard, out_weight, out_other), pick(first_shard, out_other, out_weight)],
        axis=1,
    )
    high = max(half, units)
    up_padded = jnp.pad(up_weight, ((0, high - half), (0, high - units)))
    down_padded = jnp.pad(down_weight, ((0, high - units), (0, high - half)))
    mlp_here = swap(pick(first_core, up_padded, down_padded), "shard", 1)
    mlp_there = swap(mlp_here, "ctx", 1)
    up_other = pick(first_core, mlp_here, mlp_there)[:half, :units]
    down_other = pick(first_core, mlp_there, mlp_here)[:units, :half]
    up_full = jnp.concatenate(
        [pick(first_shard, up_weight, up_other), pick(first_shard, up_other, up_weight)], axis=0
    )
    down_full = jnp.concatenate(
        [pick(first_shard, down_weight, down_other), pick(first_shard, down_other, down_weight)],
        axis=1,
    )

    rows_bf = relative(inputs[0])
    upstream = relative(cotangent[0])
    rows_count = rows_bf.shape[0]
    own_rows = rows_count // lax.axis_size("tensor")
    rows_own = rows_bf[:own_rows].astype(F32)
    upstream_own = upstream[:own_rows].astype(F32)

    attn_in = layer_norm(rows_bf.astype(F32), attn_norm_gain, attn_norm_bias).astype(BF16)
    projected = jnp.einsum("td,cdh->cth", attn_in, qkv_full, preferred_element_type=F32)
    queries = (projected[0] + query_value_bias[0]).astype(BF16)
    keys_here = projected[1].astype(BF16)
    values_here = (projected[2] + query_value_bias[1]).astype(BF16)
    queries_split = split_heads(queries)
    keys_values = jnp.concatenate([keys_here, values_here], axis=1)
    for mask in bits_of("ctx"):
        keys_values = jnp.concatenate([keys_values, swap(keys_values, "ctx", mask)], axis=0)
    keys_split = split_heads(keys_values[:, :heads_width])
    values_split = split_heads(keys_values[:, heads_width:])
    scores = (
        jnp.einsum("qhd,khd->hqk", queries_split, keys_split, preferred_element_type=F32)
        * scaling
    )
    row_max = jnp.max(scores, axis=-1, keepdims=True)
    unscaled = jnp.exp(scores - row_max)
    totals = jnp.sum(unscaled, axis=-1, keepdims=True)
    attended = (
        jnp.einsum(
            "hqk,khd->hqd", unscaled.astype(BF16), values_split, preferred_element_type=F32
        )
        / totals
    )
    log_total = row_max + jnp.log(totals)
    attended_b = (
        jnp.transpose(attended, (1, 0, 2)).reshape(rows_count, heads_width).astype(BF16)
    )
    attn_sum = reduce_scatter(product(attended_b, out_full).astype(BF16)).astype(F32)
    residual = rows_own + attn_sum + out_bias
    normed_two, norm_two_back = jax.vjp(layer_norm, residual, mlp_norm_gain, mlp_norm_bias)
    mlp_in = gather(normed_two.astype(BF16))

    d_activated = jnp.einsum("td,fd->tf", upstream, down_full, preferred_element_type=F32)
    hidden = product(mlp_in, up_full) + up_bias
    activ_f, gelu_back = jax.vjp(gelu_tanh, hidden)
    activated = activ_f.astype(BF16)
    (d_hidden,) = gelu_back(d_activated)
    up_bias_grad = jnp.sum(d_hidden, axis=0)
    d_hidden_b = d_hidden.astype(BF16)
    d_mlp_part = jnp.einsum("tf,df->td", d_hidden_b, up_full, preferred_element_type=F32)
    d_mlp_in = reduce_scatter(d_mlp_part.astype(BF16)).astype(F32)
    d_norm_two, mlp_gain_grad, mlp_shift_grad = norm_two_back(d_mlp_in)
    d_residual = upstream_own + d_norm_two
    d_residual_b = gather(d_residual.astype(BF16))

    mlp_sum = reduce_scatter(product(activated, down_full).astype(BF16), 1).astype(F32)
    output = (residual + mlp_sum + down_bias).astype(BF16)
    output_rows = relative(gather(output, 1))
    up_grad = jnp.einsum("td,tf->df", mlp_in, d_hidden_b, preferred_element_type=F32)
    down_grad = jnp.einsum("td,tf->df", upstream, activated, preferred_element_type=F32)
    up_grad = up_grad.astype(BF16)
    down_grad = down_grad.astype(BF16)
    mlp_kept = pick(first_core, up_grad, down_grad).astype(F32) + swap(
        pick(first_core, down_grad, up_grad), "ctx", 1
    ).astype(F32)
    mlp_kept = ctx_rest(mlp_kept.astype(BF16)).reshape(2, half, units)
    mlp_own = lax.dynamic_index_in_dim(mlp_kept, shard, 0, False).astype(F32) + swap(
        lax.dynamic_index_in_dim(mlp_kept, 1 - shard, 0, False), "shard", 1
    ).astype(F32)
    mlp_own = mlp_own.astype(BF16)
    mlp_pair = swap(mlp_own, "ctx", 1)
    up_owned = pick(first_core, mlp_own, mlp_pair).astype(F32)
    down_owned = jnp.transpose(pick(first_core, mlp_pair, mlp_own)).astype(F32)

    d_attended = jnp.einsum("td,hd->th", d_residual_b, out_full, preferred_element_type=F32)
    d_attended_split = split_heads(d_attended.astype(BF16))
    delta = jnp.sum(
        d_attended_split.astype(F32) * split_heads(attended_b).astype(F32), axis=-1
    )
    delta = jnp.transpose(delta)[:, :, None]
    scores_back = (
        jnp.einsum("qhd,khd->hqk", queries_split, keys_split, preferred_element_type=F32)
        * scaling
    )
    probs = jnp.exp(scores_back - log_total)
    d_probs = jnp.einsum(
        "qhd,khd->hqk", d_attended_split, values_split, preferred_element_type=F32
    )
    d_scores_b = (probs * (d_probs - delta)).astype(BF16)
    probs_b = probs.astype(BF16)
    d_queries = (
        jnp.einsum("hqk,khd->qhd", d_scores_b, keys_split, preferred_element_type=F32) * scaling
    ).reshape(rows_count, heads_width)
    key_terms = (
        jnp.einsum("hqk,qhd->khd", d_scores_b, queries_split, preferred_element_type=F32)
        * scaling
    ).reshape(-1, heads_width)
    value_terms = jnp.einsum(
        "hqk,qhd->khd", probs_b, d_attended_split, preferred_element_type=F32
    ).reshape(-1, heads_width)
    terms = jnp.concatenate([key_terms, value_terms], axis=1).astype(BF16)
    for mask in bits_of("ctx")[::-1]:
        count = terms.shape[0] // 2
        terms = (
            terms[:count].astype(F32) + swap(terms[count:], "ctx", mask).astype(F32)
        ).astype(BF16)
    kv_grad = terms.astype(F32)
    d_keys = kv_grad[:, :heads_width]
    d_values = kv_grad[:, heads_width:]
    bias_grad = jnp.stack([jnp.sum(d_queries, axis=0), jnp.sum(d_values, axis=0)])
    d_proj = jnp.stack([d_queries, d_keys, d_values]).astype(BF16)
    d_attn_part = jnp.einsum("cth,cdh->td", d_proj, qkv_full, preferred_element_type=F32)
    d_attn_in = reduce_scatter(d_attn_part.astype(BF16)).astype(F32)
    _, norm_one_back = jax.vjp(layer_norm, rows_own, attn_norm_gain, attn_norm_bias)
    d_norm_one, attn_gain_grad, attn_shift_grad = norm_one_back(d_attn_in)
    inputs_grad = (d_residual + d_norm_one).astype(BF16)
    inputs_grad_rows = relative(gather(inputs_grad)).astype(F32)

    qkv_grad = jnp.einsum("td,cth->cdh", attn_in, d_proj, preferred_element_type=F32)
    out_grad = jnp.einsum("td,th->dh", d_residual_b, attended_b, preferred_element_type=F32)
    heads_grad = jnp.concatenate([qkv_grad, out_grad[None]], axis=0).astype(BF16)
    heads_grad = heads_grad.reshape(2, 2, 2, half, heads_width)
    heads_kept = lax.dynamic_index_in_dim(heads_grad, core, 0, False).astype(F32) + swap(
        lax.dynamic_index_in_dim(heads_grad, 1 - core, 0, False), "ctx", 1
    ).astype(F32)
    heads_kept = ctx_rest(heads_kept.astype(BF16))
    heads_own = lax.dynamic_index_in_dim(heads_kept, shard, 1, False).astype(F32) + swap(
        lax.dynamic_index_in_dim(heads_kept, 1 - shard, 1, False), "shard", 1
    ).astype(F32)
    heads_own = heads_own.astype(BF16)
    heads_pair = swap(heads_own, "ctx", 1)
    low_pair = pick(first_core, heads_own, heads_pair)
    high_pair = pick(first_core, heads_pair, heads_own)
    qkv_owned = jnp.concatenate([low_pair, high_pair[:1]], axis=0).astype(F32)
    out_owned = jnp.transpose(high_pair[1]).astype(F32)

    local = jnp.concatenate([bias_grad.reshape(-1), up_bias_grad])
    local_size = local.shape[0]
    vectors = jnp.concatenate(
        [
            attn_gain_grad,
            attn_shift_grad,
            jnp.sum(d_residual, axis=0),
            mlp_gain_grad,
            mlp_shift_grad,
            jnp.sum(upstream_own, axis=0),
        ]
    )
    both = jnp.concatenate([vectors, local])
    for mask in bits_of("ctx"):
        both = both + swap(both, "ctx", mask)
    both = both + swap(both, "shard", 1)
    vectors = both[: 6 * width]
    local = both[6 * width :]
    for mask in bits_of("tensor"):
        vectors = vectors + swap(vectors, "tensor", mask)
    vectors = vectors.reshape(6, width)
    return (
        output_rows[None],
        inputs_grad_rows[None],
        vectors[0],
        vectors[1],
        qkv_owned,
        local[: 2 * heads_width].reshape(2, heads_width),
        out_owned,
        vectors[2],
        vectors[3],
        vectors[4],
        up_owned,
        local[2 * heads_width :],
        down_owned,
        vectors[5],
    )


def solution(mesh):
    in_specs = (
        P("shard", "ctx", None),
        P("shard", "ctx", None),
        P(),
        P(),
        P(None, "shard", "tensor"),
        P(None, "tensor"),
        P("tensor", "shard"),
        P(),
        P(),
        P(),
        P("shard", "tensor"),
        P("tensor"),
        P("tensor", "shard"),
        P(),
    )
    out_specs = (
        P("shard", "ctx", None),
        P("shard", "ctx", None),
        P(),
        P(),
        P(None, "shard", "tensor"),
        P(None, "tensor"),
        P("tensor", "shard"),
        P(),
        P(),
        P(),
        P("shard", "tensor"),
        P("tensor"),
        P("tensor", "shard"),
        P(),
    )
    return jax.shard_map(
        on_device, mesh=mesh, in_specs=in_specs, out_specs=out_specs, check_vma=False
    )
```

```python
import jax
import jax.numpy as jnp
from jax import lax
from jax.sharding import PartitionSpec as P

HD = 72


EPSILON = 1e-06


def layer_norm(rows, gain, shift):
    center = jnp.mean(rows, axis=-1, keepdims=True)
    offset = rows - center
    spread = jnp.mean(offset * offset, axis=-1, keepdims=True)
    return offset * lax.rsqrt(spread + EPSILON) * gain + shift


def gelu_tanh(values):
    return jax.nn.gelu(values, approximate=True)


def product(left, right):
    return jnp.dot(left, right, preferred_element_type=jnp.float32)


def split_heads(matrix):
    return matrix.reshape(matrix.shape[0], -1, HD)

BF16 = jnp.bfloat16
F32 = jnp.float32


def swap(array, axis, mask):
    count = lax.axis_size(axis)
    return lax.ppermute(array, axis, [(i, i ^ mask) for i in range(count)])


def bits_of(axis):
    count = lax.axis_size(axis)
    return [1 << b for b in range(count.bit_length() - 1)]


def take_bit(blocks, bits, mask):
    place = bits.index(mask)
    tail_shape = blocks.shape[1:]
    grid = blocks.reshape((2,) * len(bits) + tail_shape)
    low = lax.index_in_dim(grid, 0, place, False).reshape((-1,) + tail_shape)
    high = lax.index_in_dim(grid, 1, place, False).reshape((-1,) + tail_shape)
    return low, high, [b for b in bits if b != mask]


def orders_of(bits):
    first = list(bits)
    second = list(bits)
    if len(bits) > 2:
        second[0], second[1] = second[1], second[0]
    return first, second


def scatter_part(blocks, bits, order, hooks=()):
    for stage, mask in enumerate(order):
        low, high, bits = take_bit(blocks, bits, mask)
        if stage < len(hooks) and hooks[stage] is not None:
            high = after(high, hooks[stage])
        arrived = swap(high, "tensor", mask)
        blocks = (low.astype(F32) + arrived.astype(F32)).astype(BF16)
    return blocks[0]


def reduce_scatter(partial, hooks=((), ())):
    bits = bits_of("tensor")
    blocks = partial.reshape(1 << len(bits), -1, partial.shape[-1])
    step = blocks.shape[1] // 2
    done = [
        scatter_part(blocks[:, p * step : (p + 1) * step], bits[::-1], order, hooks[p])
        for p, order in enumerate(orders_of(bits))
    ]
    return jnp.concatenate(done, axis=0)


def gather_steps(block, order, hooks=()):
    blocks = block[None]
    results = []
    for stage, mask in enumerate(order):
        if stage < len(hooks) and hooks[stage] is not None:
            blocks = after(blocks, hooks[stage])
        blocks = jnp.concatenate([blocks, swap(blocks, "tensor", mask)], axis=0)
        results.append(blocks)
    return results


def in_order(blocks, order):
    bits = list(order)[::-1]
    tail_shape = blocks.shape[1:]
    grid = blocks.reshape((2,) * len(bits) + tail_shape)
    axes = [bits.index(b) for b in sorted(bits, reverse=True)]
    axes += [len(bits) + d for d in range(len(tail_shape))]
    return grid.transpose(axes).reshape((-1,) + tail_shape)


def gather(block, hooks=((), ())):
    orders = [order[::-1] for order in orders_of(bits_of("tensor"))]
    step = block.shape[0] // 2
    steps = [
        gather_steps(block[p * step : (p + 1) * step], o, hooks[p]) for p, o in enumerate(orders)
    ]
    full = jnp.concatenate([in_order(t[-1], o) for t, o in zip(steps, orders)], axis=1)
    return full, steps[0]


def norm_back(rows, gain, cotangent):
    center = jnp.mean(rows, axis=-1, keepdims=True)
    offset = rows - center
    spread = jnp.mean(offset * offset, axis=-1, keepdims=True)
    inverse = lax.rsqrt(spread + EPSILON)
    unit = offset * inverse
    scaled = cotangent * gain
    mean_one = jnp.mean(scaled, axis=-1, keepdims=True)
    mean_two = jnp.mean(scaled * unit, axis=-1, keepdims=True)
    return (
        inverse * (scaled - mean_one - unit * mean_two),
        jnp.sum(cotangent * unit, axis=0, keepdims=True),
        jnp.sum(cotangent, axis=0, keepdims=True),
    )


def transposed_product(left, right):
    return lax.dot_general(left, right, (((0,), (0,)), ((), ())), preferred_element_type=F32)


def relative(rows):
    index = lax.axis_index("tensor")
    bits = bits_of("tensor")[::-1]
    tail_shape = (rows.shape[0] >> len(bits),) + rows.shape[1:]
    grid = rows.reshape((2,) * len(bits) + tail_shape)
    for place, mask in enumerate(bits):
        grid = jnp.where((index & mask) != 0, jnp.flip(grid, place), grid)
    return grid.reshape(rows.shape)


def after(array, other):
    return lax.optimization_barrier((array, other))[0]


def pick(flag, first, second):
    return jnp.where(flag, first, second)


def ctx_rest(array):
    for mask in bits_of("ctx")[1:]:
        array = array + swap(array, "ctx", mask)
    return array


def on_device(
    inputs,
    cotangent,
    attn_norm_gain,
    attn_norm_bias,
    qkv_weight,
    query_value_bias,
    out_weight,
    out_bias,
    mlp_norm_gain,
    mlp_norm_bias,
    up_weight,
    up_bias,
    down_weight,
    down_bias,
):
    width = inputs.shape[-1]
    half = width // 2
    heads_width = qkv_weight.shape[-1]
    units = up_weight.shape[-1]
    shard = lax.axis_index("shard")
    core = lax.axis_index("ctx") & 1
    first_shard = shard == 0
    first_core = core == 0
    scaling = HD ** (-0.5)

    def own_half(array):
        return pick(first_shard, array[:, :half], array[:, half:])

    def other_half(array):
        return pick(first_shard, array[:, half:], array[:, :half])

    quarter = half // 2
    qkv_sent = lax.dynamic_slice_in_dim(qkv_weight, core * quarter, quarter, 1)
    qkv_here = swap(qkv_sent, "shard", 1)
    qkv_there = swap(qkv_here, "ctx", 1)
    qkv_other = jnp.concatenate(
        [pick(first_core, qkv_here, qkv_there), pick(first_core, qkv_there, qkv_here)], axis=1
    )
    qkv_full = jnp.concatenate(
        [pick(first_shard, qkv_weight, qkv_other), pick(first_shard, qkv_other, qkv_weight)],
        axis=1,
    )
    rows_bf = relative(inputs[0])
    upstream = relative(cotangent[0])
    rows_count = rows_bf.shape[0]
    own_rows = rows_count // lax.axis_size("tensor")
    rows_own = rows_bf[:own_rows].astype(F32)
    upstream_own = upstream[:own_rows].astype(F32)

    attn_in = layer_norm(rows_bf.astype(F32), attn_norm_gain, attn_norm_bias).astype(BF16)
    out_other = swap(after(out_weight, attn_in), "shard", 1)
    up_other = swap(after(up_weight, attn_in), "shard", 1)
    down_other = swap(after(down_weight, attn_in), "shard", 1)
    out_full = jnp.concatenate(
        [pick(first_shard, out_weight, out_other), pick(first_shard, out_other, out_weight)],
        axis=1,
    )
    projected = jnp.einsum("td,cdh->cth", attn_in, qkv_full, preferred_element_type=F32)
    queries = (projected[0] + query_value_bias[0]).astype(BF16)
    keys_here = projected[1].astype(BF16)
    values_here = (projected[2] + query_value_bias[1]).astype(BF16)
    queries_split = split_heads(queries)
    keys_values = jnp.concatenate([keys_here, values_here], axis=1)
    for mask in bits_of("ctx"):
        keys_values = jnp.concatenate([keys_values, swap(keys_values, "ctx", mask)], axis=0)
    keys_split = split_heads(keys_values[:, :heads_width])
    values_split = split_heads(keys_values[:, heads_width:])
    scores = (
        jnp.einsum("qhd,khd->hqk", queries_split, keys_split, preferred_element_type=F32)
        * scaling
    )
    row_max = jnp.max(scores, axis=-1, keepdims=True)
    unscaled = jnp.exp(scores - row_max)
    totals = jnp.sum(unscaled, axis=-1, keepdims=True)
    attended = (
        jnp.einsum(
            "hqk,khd->hqd", unscaled.astype(BF16), values_split, preferred_element_type=F32
        )
        / totals
    )
    log_total = row_max + jnp.log(totals)
    attended_b = (
        jnp.transpose(attended, (1, 0, 2)).reshape(rows_count, heads_width).astype(BF16)
    )
    attn_part = product(attended_b, out_full).astype(BF16)
    attn_sum = reduce_scatter(attn_part).astype(F32)
    residual = rows_own + attn_sum + out_bias
    normed_two = layer_norm(residual, mlp_norm_gain, mlp_norm_bias)
    mlp_in, mlp_steps = gather(normed_two.astype(BF16))
    mlp_in = mlp_in.reshape(-1, width)
    up_other = after(up_other, mlp_steps[1])
    down_other = after(down_other, mlp_steps[1])
    up_full = jnp.concatenate(
        [pick(first_shard, up_weight, up_other), pick(first_shard, up_other, up_weight)], axis=0
    )
    down_full = jnp.concatenate(
        [pick(first_shard, down_weight, down_other), pick(first_shard, down_other, down_weight)],
        axis=1,
    )

    d_activated = jnp.einsum("td,fd->tf", upstream, down_full, preferred_element_type=F32)
    hidden = product(mlp_in, up_full) + up_bias
    activ_f, gelu_back = jax.vjp(gelu_tanh, hidden)
    activated = activ_f.astype(BF16)
    (d_hidden,) = gelu_back(d_activated)
    up_bias_grad = jnp.sum(d_hidden, axis=0)
    d_hidden_b = d_hidden.astype(BF16)
    d_mlp_part = jnp.einsum("tf,df->td", d_hidden_b, up_full, preferred_element_type=F32)
    d_mlp_in = reduce_scatter(d_mlp_part.astype(BF16)).astype(F32)
    mlp_part = product(activated, down_full).astype(BF16)
    d_norm_two, mlp_gain_grad, mlp_shift_grad = norm_back(residual, mlp_norm_gain, d_mlp_in)
    d_residual = upstream_own + d_norm_two

    bits = bits_of("tensor")
    mlp_blocks = mlp_part.reshape(1 << len(bits), own_rows, width)
    low, high, left = take_bit(mlp_blocks, bits[::-1], bits[0])
    mlp_moved = swap(after(high, d_mlp_in), "tensor", bits[0])
    kept_left = pick(first_core, mlp_in, upstream)
    kept_right = pick(first_core, d_hidden_b, activated)
    sent_left = pick(first_core, upstream, mlp_in)
    sent_right = pick(first_core, activated, d_hidden_b)
    sent = [
        swap(transposed_product(h, sent_right).astype(BF16), "ctx", 1)
        for h in (other_half(sent_left), own_half(sent_left))
    ]
    kept = [
        transposed_product(h, kept_right).astype(BF16)
        for h in (other_half(kept_left), own_half(kept_left))
    ]
    d_residual_b, _ = gather(
        d_residual.astype(BF16), ((), (None, None, (mlp_moved, sent[0], kept)))
    )
    d_residual_b = d_residual_b.reshape(-1, width)

    d_attended = jnp.einsum("td,hd->th", d_residual_b, out_full, preferred_element_type=F32)
    mlp_blocks = (low.astype(F32) + mlp_moved.astype(F32)).astype(BF16)
    low, high, left = take_bit(mlp_blocks, left, bits[1])
    mlp_near = (low.astype(F32) + swap(high, "tensor", bits[1]).astype(F32)).astype(BF16)
    mlp_sum = scatter_part(mlp_near, left, bits[2:]).astype(F32)
    output = (residual + mlp_sum + down_bias).astype(BF16)
    d_attended_split = split_heads(d_attended.astype(BF16))
    delta = jnp.sum(
        d_attended_split.astype(F32) * split_heads(attended_b).astype(F32), axis=-1
    )
    delta = jnp.transpose(delta)[:, :, None]
    scores_back = (
        jnp.einsum("qhd,khd->hqk", queries_split, keys_split, preferred_element_type=F32)
        * scaling
    )
    probs = jnp.exp(scores_back - log_total)
    d_probs = jnp.einsum(
        "qhd,khd->hqk", d_attended_split, values_split, preferred_element_type=F32
    )
    d_scores_b = (probs * (d_probs - delta)).astype(BF16)
    probs_b = probs.astype(BF16)
    d_queries = (
        jnp.einsum("hqk,khd->qhd", d_scores_b, keys_split, preferred_element_type=F32) * scaling
    ).reshape(rows_count, heads_width)
    key_terms = (
        jnp.einsum(
            "hqk,qhd->khd",
            d_scores_b,
            after(queries_split, mlp_near),
            preferred_element_type=F32,
        )
        * scaling
    ).reshape(-1, heads_width)
    value_terms = jnp.einsum(
        "hqk,qhd->khd", probs_b, d_attended_split, preferred_element_type=F32
    ).reshape(-1, heads_width)
    terms = jnp.concatenate([key_terms, value_terms], axis=1).astype(BF16)
    for mask in bits_of("ctx")[::-1]:
        count = terms.shape[0] // 2
        terms = (
            terms[:count].astype(F32) + swap(terms[count:], "ctx", mask).astype(F32)
        ).astype(BF16)
    kv_grad = terms.astype(F32)
    d_keys = kv_grad[:, :heads_width]
    d_values = kv_grad[:, heads_width:]
    bias_grad = jnp.stack([jnp.sum(d_queries, axis=0), jnp.sum(d_values, axis=0)])
    d_proj = jnp.stack([d_queries, d_keys, d_values]).astype(BF16)
    d_attn_part = jnp.einsum(
        "cth,cdh->td", d_proj, qkv_full, preferred_element_type=F32
    ).astype(BF16)
    orders = [order[::-1] for order in orders_of(bits)]
    output_steps = gather_steps(after(output, d_attn_part), orders[0])
    mlp_message = kept[0].astype(F32) + after(sent[0], d_attn_part).astype(F32)
    mlp_message = ctx_rest(mlp_message.astype(BF16))
    mlp_crossed = swap(mlp_message, "shard", 1)
    mlp_own = ctx_rest((kept[1].astype(F32) + sent[1].astype(F32)).astype(BF16))
    mlp_own = (mlp_own.astype(F32) + mlp_crossed.astype(F32)).astype(BF16)
    mlp_pair = swap(mlp_own, "ctx", 1)
    up_owned = pick(first_core, mlp_own, mlp_pair).astype(F32)
    down_owned = jnp.transpose(pick(first_core, mlp_pair, mlp_own)).astype(F32)

    late = after(d_proj, d_attn_part)
    heads = []
    for part in (other_half, own_half):
        four = [transposed_product(part(attn_in), late[c]) for c in range(3)]
        four.append(transposed_product(part(d_residual_b), attended_b))
        heads.append(jnp.stack(four).astype(BF16).reshape(2, 2, half, heads_width))
    heads_kept = [pick(first_core, h[0], h[1]) for h in heads]
    heads_sent = swap(jnp.stack([pick(first_core, h[1], h[0]) for h in heads]), "ctx", 1)
    heads_message = ctx_rest(
        (heads_kept[0].astype(F32) + heads_sent[0].astype(F32)).astype(BF16)
    )
    heads_crossed = swap(heads_message, "shard", 1)
    heads_own = ctx_rest((heads_kept[1].astype(F32) + heads_sent[1].astype(F32)).astype(BF16))
    heads_own = (heads_own.astype(F32) + heads_crossed.astype(F32)).astype(BF16)
    heads_pair = swap(heads_own, "ctx", 1)
    low_pair = pick(first_core, heads_own, heads_pair)
    high_pair = pick(first_core, heads_pair, heads_own)
    qkv_owned = jnp.concatenate([low_pair, high_pair[:1]], axis=0).astype(F32)
    out_owned = jnp.transpose(high_pair[1]).astype(F32)

    d_attn_in = reduce_scatter(
        d_attn_part, ((None, (output, heads_sent), mlp_message), ((), ())[0])
    ).astype(F32)
    d_norm_one, attn_gain_grad, attn_shift_grad = norm_back(rows_own, attn_norm_gain, d_attn_in)
    inputs_grad = (d_residual + d_norm_one).astype(BF16)

    local = jnp.concatenate([bias_grad.reshape(-1), up_bias_grad])
    vectors = jnp.concatenate(
        [
            attn_gain_grad,
            attn_shift_grad,
            jnp.sum(d_residual, axis=0, keepdims=True),
            mlp_gain_grad,
            mlp_shift_grad,
            jnp.sum(upstream_own, axis=0, keepdims=True),
        ],
        axis=0,
    )
    coarse = lax.reduce_precision(vectors, 8, 7)
    blank = jnp.zeros((4, width), F32)
    extra = jnp.concatenate([coarse, vectors - coarse, blank], axis=0).astype(BF16)
    everyone, _ = gather(
        jnp.concatenate([inputs_grad, extra], axis=0),
        (
            ((output_steps[0], heads_message), (output_steps[1], mlp_crossed), None),
            (None, None, (up_owned, down_owned)),
        ),
    )
    output_rows = relative(in_order(output_steps[-1], orders[0]).reshape(-1, width))
    inputs_grad_rows = relative(everyone[:, :own_rows].reshape(-1, width)).astype(F32)
    terms = jnp.sum(everyone[:, own_rows : own_rows + 12].astype(F32), axis=0)
    both = jnp.concatenate([(terms[:6] + terms[6:]).reshape(-1), local])
    for mask in bits_of("ctx"):
        both = both + swap(both, "ctx", mask)
    both = both + swap(both, "shard", 1)
    vectors = both[: 6 * width].reshape(6, width)
    local = both[6 * width :]
    return (
        output_rows[None],
        inputs_grad_rows[None],
        vectors[0],
        vectors[1],
        qkv_owned,
        local[: 2 * heads_width].reshape(2, heads_width),
        out_owned,
        vectors[2],
        vectors[3],
        vectors[4],
        up_owned,
        local[2 * heads_width :],
        down_owned,
        vectors[5],
    )


def solution(mesh):
    in_specs = (
        P("shard", "ctx", None),
        P("shard", "ctx", None),
        P(),
        P(),
        P(None, "shard", "tensor"),
        P(None, "tensor"),
        P("tensor", "shard"),
        P(),
        P(),
        P(),
        P("shard", "tensor"),
        P("tensor"),
        P("tensor", "shard"),
        P(),
    )
    out_specs = (
        P("shard", "ctx", None),
        P("shard", "ctx", None),
        P(),
        P(),
        P(None, "shard", "tensor"),
        P(None, "tensor"),
        P("tensor", "shard"),
        P(),
        P(),
        P(),
        P("shard", "tensor"),
        P("tensor"),
        P("tensor", "shard"),
        P(),
    )
    return jax.shard_map(
        on_device, mesh=mesh, in_specs=in_specs, out_specs=out_specs, check_vma=False
    )
```

```python
import jax
import jax.numpy as jnp
from jax import lax
from jax.sharding import PartitionSpec as P

HD = 72


EPSILON = 1e-06


def layer_norm(rows, gain, shift):
    center = jnp.mean(rows, axis=-1, keepdims=True)
    offset = rows - center
    spread = jnp.mean(offset * offset, axis=-1, keepdims=True)
    return offset * lax.rsqrt(spread + EPSILON) * gain + shift


def gelu_tanh(values):
    return jax.nn.gelu(values, approximate=True)


def product(left, right):
    return jnp.dot(left, right, preferred_element_type=jnp.float32)


def split_heads(matrix):
    return matrix.reshape(matrix.shape[0], -1, HD)

BF16 = jnp.bfloat16
F32 = jnp.float32


def swap(array, axis, mask):
    count = lax.axis_size(axis)
    return lax.ppermute(array, axis, [(i, i ^ mask) for i in range(count)])


def bits_of(axis):
    count = lax.axis_size(axis)
    return [1 << b for b in range(count.bit_length() - 1)]


def take_bit(blocks, bits, mask):
    place = bits.index(mask)
    tail_shape = blocks.shape[1:]
    grid = blocks.reshape((2,) * len(bits) + tail_shape)
    low = lax.index_in_dim(grid, 0, place, False).reshape((-1,) + tail_shape)
    high = lax.index_in_dim(grid, 1, place, False).reshape((-1,) + tail_shape)
    return low, high, [b for b in bits if b != mask]


def orders_of(bits):
    first = list(bits)
    second = list(bits)
    if len(bits) > 2:
        second[0], second[1] = second[1], second[0]
    return first, second


def scatter_part(blocks, bits, order, hooks=()):
    for stage, mask in enumerate(order):
        low, high, bits = take_bit(blocks, bits, mask)
        if stage < len(hooks) and hooks[stage] is not None:
            high = after(high, hooks[stage])
        arrived = swap(high, "tensor", mask)
        blocks = (low.astype(F32) + arrived.astype(F32)).astype(BF16)
    return blocks[0]


def reduce_scatter(partial, hooks=((), ())):
    bits = bits_of("tensor")
    blocks = partial.reshape(1 << len(bits), -1, partial.shape[-1])
    step = blocks.shape[1] // 2
    done = [
        scatter_part(blocks[:, p * step : (p + 1) * step], bits[::-1], order, hooks[p])
        for p, order in enumerate(orders_of(bits))
    ]
    return jnp.concatenate(done, axis=0)


def gather_steps(block, order, hooks=()):
    blocks = block[None]
    results = []
    for stage, mask in enumerate(order):
        if stage < len(hooks) and hooks[stage] is not None:
            blocks = after(blocks, hooks[stage])
        blocks = jnp.concatenate([blocks, swap(blocks, "tensor", mask)], axis=0)
        results.append(blocks)
    return results


def in_order(blocks, order):
    bits = list(order)[::-1]
    tail_shape = blocks.shape[1:]
    grid = blocks.reshape((2,) * len(bits) + tail_shape)
    axes = [bits.index(b) for b in sorted(bits, reverse=True)]
    axes += [len(bits) + d for d in range(len(tail_shape))]
    return grid.transpose(axes).reshape((-1,) + tail_shape)


def gather(block, hooks=((), ())):
    orders = [order[::-1] for order in orders_of(bits_of("tensor"))]
    step = block.shape[0] // 2
    steps = [
        gather_steps(block[p * step : (p + 1) * step], o, hooks[p]) for p, o in enumerate(orders)
    ]
    full = jnp.concatenate([in_order(t[-1], o) for t, o in zip(steps, orders)], axis=1)
    return full, steps[0]


def norm_back(rows, gain, cotangent):
    center = jnp.mean(rows, axis=-1, keepdims=True)
    offset = rows - center
    spread = jnp.mean(offset * offset, axis=-1, keepdims=True)
    inverse = lax.rsqrt(spread + EPSILON)
    unit = offset * inverse
    scaled = cotangent * gain
    mean_one = jnp.mean(scaled, axis=-1, keepdims=True)
    mean_two = jnp.mean(scaled * unit, axis=-1, keepdims=True)
    return (
        inverse * (scaled - mean_one - unit * mean_two),
        jnp.sum(cotangent * unit, axis=0, keepdims=True),
        jnp.sum(cotangent, axis=0, keepdims=True),
    )


def transposed_product(left, right):
    return lax.dot_general(left, right, (((0,), (0,)), ((), ())), preferred_element_type=F32)


def relative(rows):
    index = lax.axis_index("tensor")
    bits = bits_of("tensor")[::-1]
    tail_shape = (rows.shape[0] >> len(bits),) + rows.shape[1:]
    grid = rows.reshape((2,) * len(bits) + tail_shape)
    for place, mask in enumerate(bits):
        grid = jnp.where((index & mask) != 0, jnp.flip(grid, place), grid)
    return grid.reshape(rows.shape)


def after(array, other):
    return lax.optimization_barrier((array, other))[0]


def pick(flag, first, second):
    return jnp.where(flag, first, second)


def ctx_rest(array):
    for mask in bits_of("ctx")[1:]:
        array = array + swap(array, "ctx", mask)
    return array


def on_device(
    inputs,
    cotangent,
    attn_norm_gain,
    attn_norm_bias,
    qkv_weight,
    query_value_bias,
    out_weight,
    out_bias,
    mlp_norm_gain,
    mlp_norm_bias,
    up_weight,
    up_bias,
    down_weight,
    down_bias,
):
    width = inputs.shape[-1]
    half = width // 2
    heads_width = qkv_weight.shape[-1]
    units = up_weight.shape[-1]
    shard = lax.axis_index("shard")
    core = lax.axis_index("ctx") & 1
    first_shard = shard == 0
    first_core = core == 0
    scaling = HD ** (-0.5)

    def own_half(array):
        return pick(first_shard, array[:, :half], array[:, half:])

    def other_half(array):
        return pick(first_shard, array[:, half:], array[:, :half])

    quarter = half // 2
    qkv_sent = lax.dynamic_slice_in_dim(qkv_weight, core * quarter, quarter, 1)
    qkv_here = swap(qkv_sent, "shard", 1)
    qkv_there = swap(qkv_here, "ctx", 1)
    qkv_other = jnp.concatenate(
        [pick(first_core, qkv_here, qkv_there), pick(first_core, qkv_there, qkv_here)], axis=1
    )
    qkv_full = jnp.concatenate(
        [pick(first_shard, qkv_weight, qkv_other), pick(first_shard, qkv_other, qkv_weight)],
        axis=1,
    )
    rows_bf = relative(inputs[0])
    upstream = relative(cotangent[0])
    rows_count = rows_bf.shape[0]
    own_rows = rows_count // lax.axis_size("tensor")
    rows_own = rows_bf[:own_rows].astype(F32)
    upstream_own = upstream[:own_rows].astype(F32)

    attn_in = layer_norm(rows_bf.astype(F32), attn_norm_gain, attn_norm_bias).astype(BF16)
    out_other = swap(after(out_weight, attn_in), "shard", 1)
    up_other = swap(after(up_weight, attn_in), "shard", 1)
    down_other = swap(after(down_weight, attn_in), "shard", 1)
    out_full = jnp.concatenate(
        [pick(first_shard, out_weight, out_other), pick(first_shard, out_other, out_weight)],
        axis=1,
    )
    projected = jnp.einsum("td,cdh->cth", attn_in, qkv_full, preferred_element_type=F32)
    queries = (projected[0] + query_value_bias[0]).astype(BF16)
    keys_here = projected[1].astype(BF16)
    values_here = (projected[2] + query_value_bias[1]).astype(BF16)
    queries_split = split_heads(queries)
    keys_values = jnp.concatenate([keys_here, values_here], axis=1)
    for mask in bits_of("ctx"):
        keys_values = jnp.concatenate([keys_values, swap(keys_values, "ctx", mask)], axis=0)
    keys_split = split_heads(keys_values[:, :heads_width])
    values_split = split_heads(keys_values[:, heads_width:])
    scores = (
        jnp.einsum("qhd,khd->hqk", queries_split, keys_split, preferred_element_type=F32)
        * scaling
    )
    row_max = jnp.max(scores, axis=-1, keepdims=True)
    unscaled = jnp.exp(scores - row_max)
    totals = jnp.sum(unscaled, axis=-1, keepdims=True)
    attended = (
        jnp.einsum(
            "hqk,khd->hqd", unscaled.astype(BF16), values_split, preferred_element_type=F32
        )
        / totals
    )
    log_total = row_max + jnp.log(totals)
    attended_b = (
        jnp.transpose(attended, (1, 0, 2)).reshape(rows_count, heads_width).astype(BF16)
    )
    attn_part = product(attended_b, out_full).astype(BF16)
    attn_sum = reduce_scatter(attn_part).astype(F32)
    residual = rows_own + attn_sum + out_bias
    normed_two = layer_norm(residual, mlp_norm_gain, mlp_norm_bias)
    mlp_in, mlp_steps = gather(normed_two.astype(BF16))
    mlp_in = mlp_in.reshape(-1, width)
    up_other = after(up_other, mlp_steps[1])
    down_other = after(down_other, mlp_steps[1])
    up_full = jnp.concatenate(
        [pick(first_shard, up_weight, up_other), pick(first_shard, up_other, up_weight)], axis=0
    )
    down_full = jnp.concatenate(
        [pick(first_shard, down_weight, down_other), pick(first_shard, down_other, down_weight)],
        axis=1,
    )

    d_activated = jnp.einsum("td,fd->tf", upstream, down_full, preferred_element_type=F32)
    hidden = product(mlp_in, up_full) + up_bias
    activ_f, gelu_back = jax.vjp(gelu_tanh, hidden)
    activated = activ_f.astype(BF16)
    (d_hidden,) = gelu_back(d_activated)
    up_bias_grad = jnp.sum(d_hidden, axis=0)
    d_hidden_b = d_hidden.astype(BF16)
    d_mlp_part = jnp.einsum("tf,df->td", d_hidden_b, up_full, preferred_element_type=F32)
    d_mlp_in = reduce_scatter(d_mlp_part.astype(BF16)).astype(F32)
    mlp_part = product(activated, down_full).astype(BF16)
    d_norm_two, mlp_gain_grad, mlp_shift_grad = norm_back(residual, mlp_norm_gain, d_mlp_in)
    d_residual = upstream_own + d_norm_two

    bits = bits_of("tensor")
    mlp_blocks = mlp_part.reshape(1 << len(bits), own_rows, width)
    low, high, left = take_bit(mlp_blocks, bits[::-1], bits[0])
    mlp_moved = swap(after(high, d_mlp_in), "tensor", bits[0])
    kept_left = pick(first_core, mlp_in, upstream)
    kept_right = pick(first_core, d_hidden_b, activated)
    sent_left = pick(first_core, upstream, mlp_in)
    sent_right = pick(first_core, activated, d_hidden_b)
    sent = [
        swap(transposed_product(h, sent_right).astype(BF16), "ctx", 1)
        for h in (other_half(sent_left), own_half(sent_left))
    ]
    kept = [
        transposed_product(h, kept_right).astype(BF16)
        for h in (other_half(kept_left), own_half(kept_left))
    ]
    d_residual_b, _ = gather(
        d_residual.astype(BF16), ((), (None, None, (mlp_moved, sent[0], kept)))
    )
    d_residual_b = d_residual_b.reshape(-1, width)

    d_attended = jnp.einsum("td,hd->th", d_residual_b, out_full, preferred_element_type=F32)
    mlp_blocks = (low.astype(F32) + mlp_moved.astype(F32)).astype(BF16)
    low, high, left = take_bit(mlp_blocks, left, bits[1])
    mlp_near = (low.astype(F32) + swap(high, "tensor", bits[1]).astype(F32)).astype(BF16)
    mlp_sum = scatter_part(mlp_near, left, bits[2:]).astype(F32)
    output = (residual + mlp_sum + down_bias).astype(BF16)
    d_attended_split = split_heads(d_attended.astype(BF16))
    delta = jnp.sum(
        d_attended_split.astype(F32) * split_heads(attended_b).astype(F32), axis=-1
    )
    delta = jnp.transpose(delta)[:, :, None]
    scores_back = (
        jnp.einsum("qhd,khd->hqk", queries_split, keys_split, preferred_element_type=F32)
        * scaling
    )
    probs = jnp.exp(scores_back - log_total)
    d_probs = jnp.einsum(
        "qhd,khd->hqk", d_attended_split, values_split, preferred_element_type=F32
    )
    d_scores_b = (probs * (d_probs - delta)).astype(BF16)
    probs_b = probs.astype(BF16)
    d_queries = (
        jnp.einsum("hqk,khd->qhd", d_scores_b, keys_split, preferred_element_type=F32) * scaling
    ).reshape(rows_count, heads_width)
    key_terms = (
        jnp.einsum(
            "hqk,qhd->khd",
            d_scores_b,
            after(queries_split, mlp_near),
            preferred_element_type=F32,
        )
        * scaling
    ).reshape(-1, heads_width)
    value_terms = jnp.einsum(
        "hqk,qhd->khd", probs_b, d_attended_split, preferred_element_type=F32
    ).reshape(-1, heads_width)
    terms = jnp.concatenate([key_terms, value_terms], axis=1).astype(BF16)
    for mask in bits_of("ctx")[::-1]:
        count = terms.shape[0] // 2
        terms = (
            terms[:count].astype(F32) + swap(terms[count:], "ctx", mask).astype(F32)
        ).astype(BF16)
    kv_grad = terms.astype(F32)
    d_keys = kv_grad[:, :heads_width]
    d_values = kv_grad[:, heads_width:]
    bias_grad = jnp.stack([jnp.sum(d_queries, axis=0), jnp.sum(d_values, axis=0)])
    d_proj = jnp.stack([d_queries, d_keys, d_values]).astype(BF16)
    d_attn_part = jnp.einsum(
        "cth,cdh->td", d_proj, qkv_full, preferred_element_type=F32
    ).astype(BF16)
    orders = [order[::-1] for order in orders_of(bits)]
    output_blocks = gather_steps(after(output, d_attn_part), orders[0][:1])[0]
    mlp_message = kept[0].astype(F32) + after(sent[0], d_attn_part).astype(F32)
    mlp_message = ctx_rest(mlp_message.astype(BF16))
    mlp_crossed = swap(mlp_message, "shard", 1)
    mlp_own = ctx_rest((kept[1].astype(F32) + sent[1].astype(F32)).astype(BF16))
    mlp_own = (mlp_own.astype(F32) + mlp_crossed.astype(F32)).astype(BF16)
    mlp_pair = swap(mlp_own, "ctx", 1)
    up_owned = pick(first_core, mlp_own, mlp_pair).astype(F32)
    down_owned = jnp.transpose(pick(first_core, mlp_pair, mlp_own)).astype(F32)

    late = after(d_proj, d_attn_part)
    heads = []
    for part in (other_half, own_half):
        three = jnp.einsum("td,cth->cdh", part(attn_in), late, preferred_element_type=F32)
        fourth = transposed_product(part(d_residual_b), attended_b)[None]
        four = jnp.concatenate([three, fourth], axis=0).astype(BF16)
        heads.append(four.reshape(2, 2, half, heads_width))
    heads_kept = [pick(first_core, h[0], h[1]) for h in heads]
    heads_sent = swap(jnp.stack([pick(first_core, h[1], h[0]) for h in heads]), "ctx", 1)
    heads_message = ctx_rest(
        (heads_kept[0].astype(F32) + heads_sent[0].astype(F32)).astype(BF16)
    )
    heads_crossed = swap(heads_message, "shard", 1)
    heads_own = ctx_rest((heads_kept[1].astype(F32) + heads_sent[1].astype(F32)).astype(BF16))
    heads_own = (heads_own.astype(F32) + heads_crossed.astype(F32)).astype(BF16)
    heads_pair = swap(heads_own, "ctx", 1)
    low_pair = pick(first_core, heads_own, heads_pair)
    high_pair = pick(first_core, heads_pair, heads_own)
    qkv_owned = jnp.concatenate([low_pair, high_pair[:1]], axis=0).astype(F32)
    out_owned = jnp.transpose(high_pair[1]).astype(F32)

    d_attn_in = reduce_scatter(
        d_attn_part, ((None, (output, heads_sent), mlp_message), ((), ())[0])
    ).astype(F32)
    output_far = output_blocks
    output_blocks = after(output_blocks, d_attn_in)
    for mask in orders[0][1:]:
        output_blocks = jnp.concatenate(
            [output_blocks, swap(output_blocks, "tensor", mask)], axis=0
        )
    d_norm_one, attn_gain_grad, attn_shift_grad = norm_back(rows_own, attn_norm_gain, d_attn_in)
    inputs_grad = (d_residual + d_norm_one).astype(BF16)

    local = jnp.concatenate([bias_grad.reshape(-1), up_bias_grad])
    vectors = jnp.concatenate(
        [
            attn_gain_grad,
            attn_shift_grad,
            jnp.sum(d_residual, axis=0, keepdims=True),
            mlp_gain_grad,
            mlp_shift_grad,
            jnp.sum(upstream_own, axis=0, keepdims=True),
        ],
        axis=0,
    )
    coarse = lax.reduce_precision(vectors, 8, 7)
    blank = jnp.zeros((4, width), F32)
    extra = jnp.concatenate([coarse, vectors - coarse, blank], axis=0).astype(BF16)
    everyone, _ = gather(
        jnp.concatenate([inputs_grad, extra], axis=0),
        (
            ((output_far, heads_message), mlp_crossed, None),
            (None, None, (up_owned, down_owned)),
        ),
    )
    output_rows = relative(in_order(output_blocks, orders[0]).reshape(-1, width))
    inputs_grad_rows = relative(everyone[:, :own_rows].reshape(-1, width)).astype(F32)
    terms = jnp.sum(everyone[:, own_rows : own_rows + 12].astype(F32), axis=0)
    both = jnp.concatenate([(terms[:6] + terms[6:]).reshape(-1), local])
    for mask in bits_of("ctx"):
        both = both + swap(both, "ctx", mask)
    both = both + swap(both, "shard", 1)
    vectors = both[: 6 * width].reshape(6, width)
    local = both[6 * width :]
    return (
        output_rows[None],
        inputs_grad_rows[None],
        vectors[0],
        vectors[1],
        qkv_owned,
        local[: 2 * heads_width].reshape(2, heads_width),
        out_owned,
        vectors[2],
        vectors[3],
        vectors[4],
        up_owned,
        local[2 * heads_width :],
        down_owned,
        vectors[5],
    )


def solution(mesh):
    in_specs = (
        P("shard", "ctx", None),
        P("shard", "ctx", None),
        P(),
        P(),
        P(None, "shard", "tensor"),
        P(None, "tensor"),
        P("tensor", "shard"),
        P(),
        P(),
        P(),
        P("shard", "tensor"),
        P("tensor"),
        P("tensor", "shard"),
        P(),
    )
    out_specs = (
        P("shard", "ctx", None),
        P("shard", "ctx", None),
        P(),
        P(),
        P(None, "shard", "tensor"),
        P(None, "tensor"),
        P("tensor", "shard"),
        P(),
        P(),
        P(),
        P("shard", "tensor"),
        P("tensor"),
        P("tensor", "shard"),
        P(),
    )
    return jax.shard_map(
        on_device, mesh=mesh, in_specs=in_specs, out_specs=out_specs, check_vma=False
    )
```

```python
import jax
import jax.numpy as jnp
from jax import lax
from jax.sharding import PartitionSpec as P

HD = 72


EPSILON = 1e-06


def layer_norm(rows, gain, shift):
    center = jnp.mean(rows, axis=-1, keepdims=True)
    offset = rows - center
    spread = jnp.mean(offset * offset, axis=-1, keepdims=True)
    return offset * lax.rsqrt(spread + EPSILON) * gain + shift


def gelu_tanh(values):
    return jax.nn.gelu(values, approximate=True)


def product(left, right):
    return jnp.dot(left, right, preferred_element_type=jnp.float32)


def split_heads(matrix):
    return matrix.reshape(matrix.shape[0], -1, HD)

BF16 = jnp.bfloat16
F32 = jnp.float32


def swap(array, axis, mask):
    count = lax.axis_size(axis)
    return lax.ppermute(array, axis, [(i, i ^ mask) for i in range(count)])


def bits_of(axis):
    count = lax.axis_size(axis)
    return [1 << b for b in range(count.bit_length() - 1)]


def take_bit(blocks, bits, mask):
    place = bits.index(mask)
    tail_shape = blocks.shape[1:]
    grid = blocks.reshape((2,) * len(bits) + tail_shape)
    low = lax.index_in_dim(grid, 0, place, False).reshape((-1,) + tail_shape)
    high = lax.index_in_dim(grid, 1, place, False).reshape((-1,) + tail_shape)
    return low, high, [b for b in bits if b != mask]


def orders_of(bits):
    first = list(bits)
    second = list(bits)
    if len(bits) > 2:
        second[0], second[1] = second[1], second[0]
    return first, second


def scatter_part(blocks, bits, order, hooks=()):
    for stage, mask in enumerate(order):
        low, high, bits = take_bit(blocks, bits, mask)
        if stage < len(hooks) and hooks[stage] is not None:
            high = after(high, hooks[stage])
        arrived = swap(high, "tensor", mask)
        blocks = (low.astype(F32) + arrived.astype(F32)).astype(BF16)
    return blocks[0]


def reduce_scatter(partial, hooks=((), ())):
    bits = bits_of("tensor")
    blocks = partial.reshape(1 << len(bits), -1, partial.shape[-1])
    step = blocks.shape[1] // 2
    done = [
        scatter_part(blocks[:, p * step : (p + 1) * step], bits[::-1], order, hooks[p])
        for p, order in enumerate(orders_of(bits))
    ]
    return jnp.concatenate(done, axis=0)


def gather_steps(block, order, hooks=()):
    blocks = block[None]
    results = []
    for stage, mask in enumerate(order):
        if stage < len(hooks) and hooks[stage] is not None:
            blocks = after(blocks, hooks[stage])
        blocks = jnp.concatenate([blocks, swap(blocks, "tensor", mask)], axis=0)
        results.append(blocks)
    return results


def in_order(blocks, order):
    bits = list(order)[::-1]
    tail_shape = blocks.shape[1:]
    grid = blocks.reshape((2,) * len(bits) + tail_shape)
    axes = [bits.index(b) for b in sorted(bits, reverse=True)]
    axes += [len(bits) + d for d in range(len(tail_shape))]
    return grid.transpose(axes).reshape((-1,) + tail_shape)


def gather(block, hooks=((), ())):
    orders = [order[::-1] for order in orders_of(bits_of("tensor"))]
    step = block.shape[0] // 2
    steps = [
        gather_steps(block[p * step : (p + 1) * step], o, hooks[p]) for p, o in enumerate(orders)
    ]
    full = jnp.concatenate([in_order(t[-1], o) for t, o in zip(steps, orders)], axis=1)
    return full, steps[0]


def norm_back(rows, gain, cotangent):
    center = jnp.mean(rows, axis=-1, keepdims=True)
    offset = rows - center
    spread = jnp.mean(offset * offset, axis=-1, keepdims=True)
    inverse = lax.rsqrt(spread + EPSILON)
    unit = offset * inverse
    scaled = cotangent * gain
    mean_one = jnp.mean(scaled, axis=-1, keepdims=True)
    mean_two = jnp.mean(scaled * unit, axis=-1, keepdims=True)
    return (
        inverse * (scaled - mean_one - unit * mean_two),
        jnp.sum(cotangent * unit, axis=0, keepdims=True),
        jnp.sum(cotangent, axis=0, keepdims=True),
    )


def transposed_product(left, right):
    return lax.dot_general(left, right, (((0,), (0,)), ((), ())), preferred_element_type=F32)


def relative(rows):
    index = lax.axis_index("tensor")
    bits = bits_of("tensor")[::-1]
    tail_shape = (rows.shape[0] >> len(bits),) + rows.shape[1:]
    grid = rows.reshape((2,) * len(bits) + tail_shape)
    for place, mask in enumerate(bits):
        grid = jnp.where((index & mask) != 0, jnp.flip(grid, place), grid)
    return grid.reshape(rows.shape)


def tie(first, second):
    return lax.optimization_barrier((first, second))


def after(array, other):
    return lax.optimization_barrier((array, other))[0]


def pick(flag, first, second):
    return jnp.where(flag, first, second)


def ctx_rest(array):
    for mask in bits_of("ctx")[1:]:
        array = array + swap(array, "ctx", mask)
    return array


def on_device(
    inputs,
    cotangent,
    attn_norm_gain,
    attn_norm_bias,
    qkv_weight,
    query_value_bias,
    out_weight,
    out_bias,
    mlp_norm_gain,
    mlp_norm_bias,
    up_weight,
    up_bias,
    down_weight,
    down_bias,
):
    width = inputs.shape[-1]
    half = width // 2
    heads_width = qkv_weight.shape[-1]
    units = up_weight.shape[-1]
    shard = lax.axis_index("shard")
    core = lax.axis_index("ctx") & 1
    first_shard = shard == 0
    first_core = core == 0
    scaling = HD ** (-0.5)

    def own_half(array):
        return pick(first_shard, array[:, :half], array[:, half:])

    def other_half(array):
        return pick(first_shard, array[:, half:], array[:, :half])

    quarter = half // 2
    qkv_sent = lax.dynamic_slice_in_dim(qkv_weight, core * quarter, quarter, 1)
    qkv_here = swap(qkv_sent, "shard", 1)
    qkv_there = swap(qkv_here, "ctx", 1)
    qkv_other = jnp.concatenate(
        [pick(first_core, qkv_here, qkv_there), pick(first_core, qkv_there, qkv_here)], axis=1
    )
    qkv_full = jnp.concatenate(
        [pick(first_shard, qkv_weight, qkv_other), pick(first_shard, qkv_other, qkv_weight)],
        axis=1,
    )
    rows_bf = relative(inputs[0])
    upstream = relative(cotangent[0])
    rows_count = rows_bf.shape[0]
    own_rows = rows_count // lax.axis_size("tensor")
    rows_own = rows_bf[:own_rows].astype(F32)
    upstream_own = upstream[:own_rows].astype(F32)

    attn_in = layer_norm(rows_bf.astype(F32), attn_norm_gain, attn_norm_bias).astype(BF16)
    out_other = swap(after(out_weight, attn_in), "shard", 1)
    up_other = swap(after(up_weight, attn_in), "shard", 1)
    down_other = swap(after(down_weight, attn_in), "shard", 1)
    out_full = jnp.concatenate(
        [pick(first_shard, out_weight, out_other), pick(first_shard, out_other, out_weight)],
        axis=1,
    )
    projected = jnp.einsum("td,cdh->cth", attn_in, qkv_full, preferred_element_type=F32)
    queries = (projected[0] + query_value_bias[0]).astype(BF16)
    keys_here = projected[1].astype(BF16)
    values_here = (projected[2] + query_value_bias[1]).astype(BF16)
    queries_split = split_heads(queries)
    keys_values = jnp.concatenate([keys_here, values_here], axis=1)
    for mask in bits_of("ctx"):
        keys_values = jnp.concatenate([keys_values, swap(keys_values, "ctx", mask)], axis=0)
    keys_split = split_heads(keys_values[:, :heads_width])
    values_split = split_heads(keys_values[:, heads_width:])
    scores = (
        jnp.einsum("qhd,khd->hqk", queries_split, keys_split, preferred_element_type=F32)
        * scaling
    )
    row_max = jnp.max(scores, axis=-1, keepdims=True)
    unscaled = jnp.exp(scores - row_max)
    totals = jnp.sum(unscaled, axis=-1, keepdims=True)
    attended = (
        jnp.einsum(
            "hqk,khd->hqd", unscaled.astype(BF16), values_split, preferred_element_type=F32
        )
        / totals
    )
    log_total = row_max + jnp.log(totals)
    attended_b = (
        jnp.transpose(attended, (1, 0, 2)).reshape(rows_count, heads_width).astype(BF16)
    )
    attn_part = product(attended_b, out_full).astype(BF16)
    attn_sum = reduce_scatter(attn_part).astype(F32)
    residual = rows_own + attn_sum + out_bias
    normed_two = layer_norm(residual, mlp_norm_gain, mlp_norm_bias)
    mlp_in, mlp_steps = gather(normed_two.astype(BF16))
    mlp_in = mlp_in.reshape(-1, width)
    up_other = after(up_other, mlp_steps[1])
    down_other = after(down_other, mlp_steps[1])
    up_full = jnp.concatenate(
        [pick(first_shard, up_weight, up_other), pick(first_shard, up_other, up_weight)], axis=0
    )
    down_full = jnp.concatenate(
        [pick(first_shard, down_weight, down_other), pick(first_shard, down_other, down_weight)],
        axis=1,
    )

    d_activated = jnp.einsum("td,fd->tf", upstream, down_full, preferred_element_type=F32)
    hidden = product(mlp_in, up_full) + up_bias
    activ_f, gelu_back = jax.vjp(gelu_tanh, hidden)
    activated = activ_f.astype(BF16)
    (d_hidden,) = gelu_back(d_activated)
    up_bias_grad = jnp.sum(d_hidden, axis=0)
    d_hidden_b = d_hidden.astype(BF16)
    d_mlp_part = jnp.einsum("tf,df->td", d_hidden_b, up_full, preferred_element_type=F32)
    d_mlp_in = reduce_scatter(d_mlp_part.astype(BF16)).astype(F32)
    mlp_part = product(activated, down_full).astype(BF16)
    d_norm_two, mlp_gain_grad, mlp_shift_grad = norm_back(residual, mlp_norm_gain, d_mlp_in)
    d_residual = upstream_own + d_norm_two

    bits = bits_of("tensor")
    mlp_blocks = mlp_part.reshape(1 << len(bits), own_rows, width)
    low, high, left = take_bit(mlp_blocks, bits[::-1], bits[0])
    mlp_moved = swap(high, "tensor", bits[0])
    kept_left = pick(first_core, mlp_in, upstream)
    kept_right = pick(first_core, d_hidden_b, activated)
    sent_left = pick(first_core, upstream, mlp_in)
    sent_right = pick(first_core, activated, d_hidden_b)
    sent = [
        swap(transposed_product(h, sent_right).astype(BF16), "ctx", 1)
        for h in (other_half(sent_left), own_half(sent_left))
    ]
    kept = [
        transposed_product(h, kept_right).astype(BF16)
        for h in (other_half(kept_left), own_half(kept_left))
    ]
    d_residual_b, _ = gather(
        d_residual.astype(BF16), ((), (None, None, (mlp_moved, sent[0], kept)))
    )
    d_residual_b = d_residual_b.reshape(-1, width)

    d_attended = jnp.einsum("td,hd->th", d_residual_b, out_full, preferred_element_type=F32)
    mlp_moved, d_residual_late = tie(mlp_moved, d_residual_b)
    mlp_blocks = (low.astype(F32) + mlp_moved.astype(F32)).astype(BF16)
    low, high, left = take_bit(mlp_blocks, left, bits[1])
    mlp_near = (low.astype(F32) + swap(high, "tensor", bits[1]).astype(F32)).astype(BF16)
    mlp_sum = scatter_part(mlp_near, left, bits[2:]).astype(F32)
    output = (residual + mlp_sum + down_bias).astype(BF16)
    d_attended_split = split_heads(d_attended.astype(BF16))
    delta = jnp.sum(
        d_attended_split.astype(F32) * split_heads(attended_b).astype(F32), axis=-1
    )
    delta = jnp.transpose(delta)[:, :, None]
    scores_back = (
        jnp.einsum("qhd,khd->hqk", queries_split, keys_split, preferred_element_type=F32)
        * scaling
    )
    probs = jnp.exp(scores_back - log_total)
    d_probs = jnp.einsum(
        "qhd,khd->hqk", d_attended_split, values_split, preferred_element_type=F32
    )
    d_scores_b = (probs * (d_probs - delta)).astype(BF16)
    probs_b = probs.astype(BF16)
    d_queries = (
        jnp.einsum("hqk,khd->qhd", d_scores_b, keys_split, preferred_element_type=F32) * scaling
    ).reshape(rows_count, heads_width)
    key_terms = (
        jnp.einsum(
            "hqk,qhd->khd",
            d_scores_b,
            queries_split,
            preferred_element_type=F32,
        )
        * scaling
    ).reshape(-1, heads_width)
    value_terms = jnp.einsum(
        "hqk,qhd->khd", probs_b, d_attended_split, preferred_element_type=F32
    ).reshape(-1, heads_width)
    terms = jnp.concatenate([key_terms, value_terms], axis=1).astype(BF16)
    for mask in bits_of("ctx")[::-1]:
        count = terms.shape[0] // 2
        terms = (
            terms[:count].astype(F32) + swap(terms[count:], "ctx", mask).astype(F32)
        ).astype(BF16)
    kv_grad = terms.astype(F32)
    d_keys = kv_grad[:, :heads_width]
    d_values = kv_grad[:, heads_width:]
    bias_grad = jnp.stack([jnp.sum(d_queries, axis=0), jnp.sum(d_values, axis=0)])
    d_proj = jnp.stack([d_queries, d_keys, d_values]).astype(BF16)
    d_attn_part = jnp.einsum(
        "cth,cdh->td", d_proj, qkv_full, preferred_element_type=F32
    ).astype(BF16)
    orders = [order[::-1] for order in orders_of(bits)]
    output_blocks = gather_steps(after(output, d_attn_part), orders[0][:1])[0]
    mlp_message = kept[0].astype(F32) + after(sent[0], d_attn_part).astype(F32)
    mlp_message = ctx_rest(mlp_message.astype(BF16))
    mlp_crossed = swap(mlp_message, "shard", 1)
    mlp_own = ctx_rest((kept[1].astype(F32) + sent[1].astype(F32)).astype(BF16))
    mlp_own = (mlp_own.astype(F32) + mlp_crossed.astype(F32)).astype(BF16)
    mlp_pair = swap(mlp_own, "ctx", 1)
    up_owned = pick(first_core, mlp_own, mlp_pair).astype(F32)
    down_owned = jnp.transpose(pick(first_core, mlp_pair, mlp_own)).astype(F32)

    late = after(d_proj, d_attn_part)
    heads = []
    for part in (other_half, own_half):
        three = jnp.einsum("td,cth->cdh", part(attn_in), late, preferred_element_type=F32)
        fourth = transposed_product(part(d_residual_late), attended_b)[None]
        four = jnp.concatenate([three, fourth], axis=0).astype(BF16)
        heads.append(four.reshape(2, 2, half, heads_width))
    heads_kept = [pick(first_core, h[0], h[1]) for h in heads]
    heads_sent = swap(jnp.stack([pick(first_core, h[1], h[0]) for h in heads]), "ctx", 1)
    heads_message = ctx_rest(
        (heads_kept[0].astype(F32) + heads_sent[0].astype(F32)).astype(BF16)
    )
    heads_crossed = swap(heads_message, "shard", 1)
    heads_own = ctx_rest((heads_kept[1].astype(F32) + heads_sent[1].astype(F32)).astype(BF16))
    heads_own = (heads_own.astype(F32) + heads_crossed.astype(F32)).astype(BF16)
    heads_pair = swap(heads_own, "ctx", 1)
    low_pair = pick(first_core, heads_own, heads_pair)
    high_pair = pick(first_core, heads_pair, heads_own)
    qkv_owned = jnp.concatenate([low_pair, high_pair[:1]], axis=0).astype(F32)
    out_owned = jnp.transpose(high_pair[1]).astype(F32)

    d_attn_in = reduce_scatter(
        d_attn_part, ((None, (output, heads_sent), mlp_message), ((), ())[0])
    ).astype(F32)
    output_far = output_blocks
    output_blocks = after(output_blocks, d_attn_in)
    for mask in orders[0][1:]:
        output_blocks = jnp.concatenate(
            [output_blocks, swap(output_blocks, "tensor", mask)], axis=0
        )
    d_norm_one, attn_gain_grad, attn_shift_grad = norm_back(rows_own, attn_norm_gain, d_attn_in)
    inputs_grad = (d_residual + d_norm_one).astype(BF16)

    local = jnp.concatenate([bias_grad.reshape(-1), up_bias_grad])
    vectors = jnp.concatenate(
        [
            attn_gain_grad,
            attn_shift_grad,
            jnp.sum(d_residual, axis=0, keepdims=True),
            mlp_gain_grad,
            mlp_shift_grad,
            jnp.sum(upstream_own, axis=0, keepdims=True),
        ],
        axis=0,
    )
    coarse = lax.reduce_precision(vectors, 8, 7)
    blank = jnp.zeros((4, width), F32)
    extra = jnp.concatenate([coarse, vectors - coarse, blank], axis=0).astype(BF16)
    everyone, final_steps = gather(
        jnp.concatenate([extra, inputs_grad], axis=0),
        (
            ((output_far, heads_message), mlp_crossed, None),
            (None, None, (up_owned, down_owned)),
        ),
    )
    output_rows = relative(in_order(output_blocks, orders[0]).reshape(-1, width))
    inputs_grad_rows = relative(everyone[:, 16:].reshape(-1, width)).astype(F32)
    terms = jnp.sum(final_steps[-1][:, :12].astype(F32), axis=0)
    both = jnp.concatenate([(terms[:6] + terms[6:]).reshape(-1), local])
    for mask in bits_of("ctx"):
        both = both + swap(both, "ctx", mask)
    both = both + swap(both, "shard", 1)
    vectors = both[: 6 * width].reshape(6, width)
    local = both[6 * width :]
    return (
        output_rows[None],
        inputs_grad_rows[None],
        vectors[0],
        vectors[1],
        qkv_owned,
        local[: 2 * heads_width].reshape(2, heads_width),
        out_owned,
        vectors[2],
        vectors[3],
        vectors[4],
        up_owned,
        local[2 * heads_width :],
        down_owned,
        vectors[5],
    )


def solution(mesh):
    in_specs = (
        P("shard", "ctx", None),
        P("shard", "ctx", None),
        P(),
        P(),
        P(None, "shard", "tensor"),
        P(None, "tensor"),
        P("tensor", "shard"),
        P(),
        P(),
        P(),
        P("shard", "tensor"),
        P("tensor"),
        P("tensor", "shard"),
        P(),
    )
    out_specs = (
        P("shard", "ctx", None),
        P("shard", "ctx", None),
        P(),
        P(),
        P(None, "shard", "tensor"),
        P(None, "tensor"),
        P("tensor", "shard"),
        P(),
        P(),
        P(),
        P("shard", "tensor"),
        P("tensor"),
        P("tensor", "shard"),
        P(),
    )
    return jax.shard_map(
        on_device, mesh=mesh, in_specs=in_specs, out_specs=out_specs, check_vma=False
    )
```

```python
import jax
import jax.numpy as jnp
from jax import lax
from jax.sharding import PartitionSpec as P

HD = 72


EPSILON = 1e-06


def layer_norm(rows, gain, shift):
    center = jnp.mean(rows, axis=-1, keepdims=True)
    offset = rows - center
    spread = jnp.mean(offset * offset, axis=-1, keepdims=True)
    return offset * lax.rsqrt(spread + EPSILON) * gain + shift


def gelu_tanh(values):
    return jax.nn.gelu(values, approximate=True)


def product(left, right):
    return jnp.dot(left, right, preferred_element_type=jnp.float32)


def split_heads(matrix):
    return matrix.reshape(matrix.shape[0], -1, HD)

BF16 = jnp.bfloat16
F32 = jnp.float32


def swap(array, axis, mask):
    count = lax.axis_size(axis)
    return lax.ppermute(array, axis, [(i, i ^ mask) for i in range(count)])


def bits_of(axis):
    count = lax.axis_size(axis)
    return [1 << b for b in range(count.bit_length() - 1)]


def take_bit(blocks, bits, mask):
    place = bits.index(mask)
    tail_shape = blocks.shape[1:]
    grid = blocks.reshape((2,) * len(bits) + tail_shape)
    low = lax.index_in_dim(grid, 0, place, False).reshape((-1,) + tail_shape)
    high = lax.index_in_dim(grid, 1, place, False).reshape((-1,) + tail_shape)
    return low, high, [b for b in bits if b != mask]


def orders_of(bits):
    first = list(bits)
    second = list(bits)
    if len(bits) > 2:
        second[0], second[1] = second[1], second[0]
    return first, second


def scatter_part(blocks, bits, order, hooks=()):
    for stage, mask in enumerate(order):
        low, high, bits = take_bit(blocks, bits, mask)
        if stage < len(hooks) and hooks[stage] is not None:
            high = after(high, hooks[stage])
        arrived = swap(high, "tensor", mask)
        blocks = (low.astype(F32) + arrived.astype(F32)).astype(BF16)
    return blocks[0]


def reduce_scatter(partial, hooks=((), ())):
    bits = bits_of("tensor")
    blocks = partial.reshape(1 << len(bits), -1, partial.shape[-1])
    step = blocks.shape[1] // 2
    done = [
        scatter_part(blocks[:, p * step : (p + 1) * step], bits[::-1], order, hooks[p])
        for p, order in enumerate(orders_of(bits))
    ]
    return jnp.concatenate(done, axis=0)


def gather_steps(block, order, hooks=()):
    blocks = block[None]
    results = []
    for stage, mask in enumerate(order):
        if stage < len(hooks) and hooks[stage] is not None:
            blocks = after(blocks, hooks[stage])
        blocks = jnp.concatenate([blocks, swap(blocks, "tensor", mask)], axis=0)
        results.append(blocks)
    return results


def in_order(blocks, order):
    bits = list(order)[::-1]
    tail_shape = blocks.shape[1:]
    grid = blocks.reshape((2,) * len(bits) + tail_shape)
    axes = [bits.index(b) for b in sorted(bits, reverse=True)]
    axes += [len(bits) + d for d in range(len(tail_shape))]
    return grid.transpose(axes).reshape((-1,) + tail_shape)


def gather(block, hooks=((), ())):
    orders = [order[::-1] for order in orders_of(bits_of("tensor"))]
    step = block.shape[0] // 2
    steps = [
        gather_steps(block[p * step : (p + 1) * step], o, hooks[p]) for p, o in enumerate(orders)
    ]
    full = jnp.concatenate([in_order(t[-1], o) for t, o in zip(steps, orders)], axis=1)
    return full, steps[0]


def norm_back(rows, gain, cotangent):
    center = jnp.mean(rows, axis=-1, keepdims=True)
    offset = rows - center
    spread = jnp.mean(offset * offset, axis=-1, keepdims=True)
    inverse = lax.rsqrt(spread + EPSILON)
    unit = offset * inverse
    scaled = cotangent * gain
    mean_one = jnp.mean(scaled, axis=-1, keepdims=True)
    mean_two = jnp.mean(scaled * unit, axis=-1, keepdims=True)
    return (
        inverse * (scaled - mean_one - unit * mean_two),
        jnp.sum(cotangent * unit, axis=0, keepdims=True),
        jnp.sum(cotangent, axis=0, keepdims=True),
    )


def transposed_product(left, right):
    return lax.dot_general(left, right, (((0,), (0,)), ((), ())), preferred_element_type=F32)


def relative(rows):
    index = lax.axis_index("tensor")
    bits = bits_of("tensor")[::-1]
    tail_shape = (rows.shape[0] >> len(bits),) + rows.shape[1:]
    grid = rows.reshape((2,) * len(bits) + tail_shape)
    for place, mask in enumerate(bits):
        grid = jnp.where((index & mask) != 0, jnp.flip(grid, place), grid)
    return grid.reshape(rows.shape)


def tie(first, second):
    return lax.optimization_barrier((first, second))


def after(array, other):
    return lax.optimization_barrier((array, other))[0]


def pick(flag, first, second):
    return jnp.where(flag, first, second)


def ctx_rest(array):
    for mask in bits_of("ctx")[1:]:
        array = array + swap(array, "ctx", mask)
    return array


def on_device(
    inputs,
    cotangent,
    attn_norm_gain,
    attn_norm_bias,
    qkv_weight,
    query_value_bias,
    out_weight,
    out_bias,
    mlp_norm_gain,
    mlp_norm_bias,
    up_weight,
    up_bias,
    down_weight,
    down_bias,
):
    width = inputs.shape[-1]
    half = width // 2
    heads_width = qkv_weight.shape[-1]
    units = up_weight.shape[-1]
    shard = lax.axis_index("shard")
    core = lax.axis_index("ctx") & 1
    first_shard = shard == 0
    first_core = core == 0
    scaling = HD ** (-0.5)

    def own_half(array):
        return pick(first_shard, array[:, :half], array[:, half:])

    def other_half(array):
        return pick(first_shard, array[:, half:], array[:, :half])

    quarter = half // 2
    qkv_sent = lax.dynamic_slice_in_dim(qkv_weight, core * quarter, quarter, 1)
    qkv_here = swap(qkv_sent, "shard", 1)
    qkv_there = swap(qkv_here, "ctx", 1)
    qkv_other = jnp.concatenate(
        [pick(first_core, qkv_here, qkv_there), pick(first_core, qkv_there, qkv_here)], axis=1
    )
    qkv_full = jnp.concatenate(
        [pick(first_shard, qkv_weight, qkv_other), pick(first_shard, qkv_other, qkv_weight)],
        axis=1,
    )
    rows_bf = relative(inputs[0])
    upstream = relative(cotangent[0])
    rows_count = rows_bf.shape[0]
    own_rows = rows_count // lax.axis_size("tensor")
    rows_own = rows_bf[:own_rows].astype(F32)
    upstream_own = upstream[:own_rows].astype(F32)

    attn_in = layer_norm(rows_bf.astype(F32), attn_norm_gain, attn_norm_bias).astype(BF16)
    out_other = swap(after(out_weight, attn_in), "shard", 1)
    up_other = swap(after(up_weight, attn_in), "shard", 1)
    down_other = swap(after(down_weight, attn_in), "shard", 1)
    out_full = jnp.concatenate(
        [pick(first_shard, out_weight, out_other), pick(first_shard, out_other, out_weight)],
        axis=1,
    )
    projected = jnp.einsum("td,cdh->cth", attn_in, qkv_full, preferred_element_type=F32)
    queries = (projected[0] + query_value_bias[0]).astype(BF16)
    keys_here = projected[1].astype(BF16)
    values_here = (projected[2] + query_value_bias[1]).astype(BF16)
    queries_split = split_heads(queries)
    keys_values = jnp.concatenate([keys_here, values_here], axis=1)
    for mask in bits_of("ctx"):
        keys_values = jnp.concatenate([keys_values, swap(keys_values, "ctx", mask)], axis=0)
    keys_split = split_heads(keys_values[:, :heads_width])
    values_split = split_heads(keys_values[:, heads_width:])
    scores = (
        jnp.einsum("qhd,khd->hqk", queries_split, keys_split, preferred_element_type=F32)
        * scaling
    )
    row_max = jnp.max(scores, axis=-1, keepdims=True)
    unscaled = jnp.exp(scores - row_max)
    totals = jnp.sum(unscaled, axis=-1, keepdims=True)
    attended = (
        jnp.einsum(
            "hqk,khd->hqd", unscaled.astype(BF16), values_split, preferred_element_type=F32
        )
        / totals
    )
    log_total = row_max + jnp.log(totals)
    attended_b = (
        jnp.transpose(attended, (1, 0, 2)).reshape(rows_count, heads_width).astype(BF16)
    )
    attn_part = product(attended_b, out_full).astype(BF16)
    attn_sum = reduce_scatter(attn_part).astype(F32)
    residual = rows_own + attn_sum + out_bias
    normed_two = layer_norm(residual, mlp_norm_gain, mlp_norm_bias)
    mlp_in, mlp_steps = gather(normed_two.astype(BF16))
    mlp_in = mlp_in.reshape(-1, width)
    up_other = after(up_other, mlp_steps[1])
    down_other = after(down_other, mlp_steps[1])
    up_full = jnp.concatenate(
        [pick(first_shard, up_weight, up_other), pick(first_shard, up_other, up_weight)], axis=0
    )
    down_full = jnp.concatenate(
        [pick(first_shard, down_weight, down_other), pick(first_shard, down_other, down_weight)],
        axis=1,
    )

    d_activated = jnp.einsum("td,fd->tf", upstream, down_full, preferred_element_type=F32)
    hidden = product(mlp_in, up_full) + up_bias
    activ_f, gelu_back = jax.vjp(gelu_tanh, hidden)
    activated = activ_f.astype(BF16)
    (d_hidden,) = gelu_back(d_activated)
    up_bias_grad = jnp.sum(d_hidden, axis=0)
    d_hidden_b = d_hidden.astype(BF16)
    d_mlp_part = jnp.einsum("tf,df->td", d_hidden_b, up_full, preferred_element_type=F32)
    d_mlp_in = reduce_scatter(d_mlp_part.astype(BF16)).astype(F32)
    mlp_part = product(activated, down_full).astype(BF16)
    d_norm_two, mlp_gain_grad, mlp_shift_grad = norm_back(residual, mlp_norm_gain, d_mlp_in)
    d_residual = upstream_own + d_norm_two

    bits = bits_of("tensor")
    mlp_blocks = mlp_part.reshape(1 << len(bits), own_rows, width)
    low, high, left = take_bit(mlp_blocks, bits[::-1], bits[0])
    mlp_moved = swap(high, "tensor", bits[0])
    kept_left = pick(first_core, mlp_in, upstream)
    kept_right = pick(first_core, d_hidden_b, activated)
    sent_left = pick(first_core, upstream, mlp_in)
    sent_right = pick(first_core, activated, d_hidden_b)
    sent = [
        swap(transposed_product(h, sent_right).astype(BF16), "ctx", 1)
        for h in (other_half(sent_left), own_half(sent_left))
    ]
    kept = [
        transposed_product(h, kept_right).astype(BF16)
        for h in (other_half(kept_left), own_half(kept_left))
    ]
    d_residual_b, _ = gather(
        d_residual.astype(BF16), ((), (None, None, (mlp_moved, sent[0], kept)))
    )
    d_residual_b = d_residual_b.reshape(-1, width)

    d_attended = jnp.einsum("td,hd->th", d_residual_b, out_full, preferred_element_type=F32)
    mlp_moved, d_residual_late = tie(mlp_moved, d_residual_b)
    mlp_blocks = (low.astype(F32) + mlp_moved.astype(F32)).astype(BF16)
    low, high, left = take_bit(mlp_blocks, left, bits[1])
    mlp_near = (low.astype(F32) + swap(high, "tensor", bits[1]).astype(F32)).astype(BF16)
    mlp_sum = scatter_part(mlp_near, left, bits[2:]).astype(F32)
    output = (residual + mlp_sum + down_bias).astype(BF16)
    d_attended_split = split_heads(d_attended.astype(BF16))
    delta = jnp.sum(
        d_attended_split.astype(F32) * split_heads(attended_b).astype(F32), axis=-1
    )
    delta = jnp.transpose(delta)[:, :, None]
    scores_back = (
        jnp.einsum("qhd,khd->hqk", queries_split, keys_split, preferred_element_type=F32)
        * scaling
    )
    probs = jnp.exp(scores_back - log_total)
    d_probs = jnp.einsum(
        "qhd,khd->hqk", d_attended_split, values_split, preferred_element_type=F32
    )
    d_scores_b = (probs * (d_probs - delta)).astype(BF16)
    probs_b = probs.astype(BF16)
    d_queries = (
        jnp.einsum("hqk,khd->qhd", d_scores_b, keys_split, preferred_element_type=F32) * scaling
    ).reshape(rows_count, heads_width)
    key_terms = (
        jnp.einsum(
            "hqk,qhd->khd",
            d_scores_b,
            queries_split,
            preferred_element_type=F32,
        )
        * scaling
    ).reshape(-1, heads_width)
    value_terms = jnp.einsum(
        "hqk,qhd->khd", probs_b, d_attended_split, preferred_element_type=F32
    ).reshape(-1, heads_width)
    terms = jnp.concatenate([key_terms, value_terms], axis=1).astype(BF16)
    for mask in bits_of("ctx")[::-1]:
        count = terms.shape[0] // 2
        terms = (
            terms[:count].astype(F32) + swap(terms[count:], "ctx", mask).astype(F32)
        ).astype(BF16)
    kv_grad = terms.astype(F32)
    d_keys = kv_grad[:, :heads_width]
    d_values = kv_grad[:, heads_width:]
    bias_grad = jnp.stack([jnp.sum(d_queries, axis=0), jnp.sum(d_values, axis=0)])
    d_proj = jnp.stack([d_queries, d_keys, d_values]).astype(BF16)
    d_attn_part = jnp.einsum(
        "cth,cdh->td", d_proj, qkv_full, preferred_element_type=F32
    ).astype(BF16)
    orders = [order[::-1] for order in orders_of(bits)]
    output_blocks = gather_steps(after(output, d_attn_part), orders[0][:1])[0]
    mlp_message = kept[0].astype(F32) + after(sent[0], d_attn_part).astype(F32)
    mlp_message = ctx_rest(mlp_message.astype(BF16))
    mlp_crossed = swap(mlp_message, "shard", 1)
    mlp_own = ctx_rest((kept[1].astype(F32) + sent[1].astype(F32)).astype(BF16))
    mlp_own = (mlp_own.astype(F32) + mlp_crossed.astype(F32)).astype(BF16)
    mlp_pair = swap(mlp_own, "ctx", 1)
    up_owned = pick(first_core, mlp_own, mlp_pair).astype(F32)
    down_owned = jnp.transpose(pick(first_core, mlp_pair, mlp_own)).astype(F32)

    late = after(d_proj, d_attn_part)
    heads = []
    for part in (other_half, own_half):
        three = jnp.einsum("td,cth->cdh", part(attn_in), late, preferred_element_type=F32)
        fourth = transposed_product(part(d_residual_late), attended_b)[None]
        four = jnp.concatenate([three, fourth], axis=0).astype(BF16)
        heads.append(four.reshape(2, 2, half, heads_width))
    heads_kept = [pick(first_core, h[0], h[1]) for h in heads]
    heads_sent = swap(jnp.stack([pick(first_core, h[1], h[0]) for h in heads]), "ctx", 1)
    heads_message = ctx_rest(
        (heads_kept[0].astype(F32) + heads_sent[0].astype(F32)).astype(BF16)
    )
    heads_crossed = swap(heads_message, "shard", 1)
    heads_own = ctx_rest((heads_kept[1].astype(F32) + heads_sent[1].astype(F32)).astype(BF16))
    heads_own = (heads_own.astype(F32) + heads_crossed.astype(F32)).astype(BF16)
    heads_pair = swap(heads_own, "ctx", 1)
    low_pair = pick(first_core, heads_own, heads_pair)
    high_pair = pick(first_core, heads_pair, heads_own)
    qkv_owned = jnp.concatenate([low_pair, high_pair[:1]], axis=0).astype(F32)
    out_owned = jnp.transpose(high_pair[1]).astype(F32)

    d_attn_in = reduce_scatter(
        d_attn_part, ((None, heads_sent, mlp_message), ((), ())[0])
    ).astype(F32)
    output_far = output_blocks
    output_blocks = after(output_blocks, d_attn_in)
    for mask in orders[0][1:]:
        output_blocks = jnp.concatenate(
            [output_blocks, swap(output_blocks, "tensor", mask)], axis=0
        )
    d_norm_one, attn_gain_grad, attn_shift_grad = norm_back(rows_own, attn_norm_gain, d_attn_in)
    inputs_grad = (d_residual + d_norm_one).astype(BF16)

    local = jnp.concatenate([bias_grad.reshape(-1), up_bias_grad])
    vectors = jnp.concatenate(
        [
            attn_gain_grad,
            attn_shift_grad,
            jnp.sum(d_residual, axis=0, keepdims=True),
            mlp_gain_grad,
            mlp_shift_grad,
            jnp.sum(upstream_own, axis=0, keepdims=True),
        ],
        axis=0,
    )
    coarse = lax.reduce_precision(vectors, 8, 7)
    blank = jnp.zeros((4, width), F32)
    extra = jnp.concatenate([coarse, vectors - coarse, blank], axis=0).astype(BF16)
    everyone, final_steps = gather(
        jnp.concatenate([extra, inputs_grad], axis=0),
        (
            ((output_far, heads_message), mlp_crossed, None),
            (None, None, (up_owned, down_owned)),
        ),
    )
    output_rows = relative(in_order(output_blocks, orders[0]).reshape(-1, width))
    inputs_grad_rows = relative(everyone[:, 16:].reshape(-1, width)).astype(F32)
    terms = jnp.sum(final_steps[-1][:, :12].astype(F32), axis=0)
    both = jnp.concatenate([(terms[:6] + terms[6:]).reshape(-1), local])
    for mask in bits_of("ctx"):
        both = both + swap(both, "ctx", mask)
    both = both + swap(both, "shard", 1)
    vectors = both[: 6 * width].reshape(6, width)
    local = both[6 * width :]
    return (
        output_rows[None],
        inputs_grad_rows[None],
        vectors[0],
        vectors[1],
        qkv_owned,
        local[: 2 * heads_width].reshape(2, heads_width),
        out_owned,
        vectors[2],
        vectors[3],
        vectors[4],
        up_owned,
        local[2 * heads_width :],
        down_owned,
        vectors[5],
    )


def solution(mesh):
    in_specs = (
        P("shard", "ctx", None),
        P("shard", "ctx", None),
        P(),
        P(),
        P(None, "shard", "tensor"),
        P(None, "tensor"),
        P("tensor", "shard"),
        P(),
        P(),
        P(),
        P("shard", "tensor"),
        P("tensor"),
        P("tensor", "shard"),
        P(),
    )
    out_specs = (
        P("shard", "ctx", None),
        P("shard", "ctx", None),
        P(),
        P(),
        P(None, "shard", "tensor"),
        P(None, "tensor"),
        P("tensor", "shard"),
        P(),
        P(),
        P(),
        P("shard", "tensor"),
        P("tensor"),
        P("tensor", "shard"),
        P(),
    )
    return jax.shard_map(
        on_device, mesh=mesh, in_specs=in_specs, out_specs=out_specs, check_vma=False
    )
```
